32 devices in a mesh: ctx: 16 (over z, x, core), dp: 2 (over y).
Axes of the slice: x: 2, y: 2, z: 4, core: 2. Of those that a mesh axis runs over, the one named last changes fastest.
Arguments:
- query_proj: bfloat16 [2, 2048, 1024], P('dp', 'ctx'), may hold values from -6 to 6
- key_proj: bfloat16 [2, 2048, 1024], P('dp', 'ctx'), may hold values from -6 to 6
- value_proj: bfloat16 [2, 2048, 1024], P('dp', 'ctx'), may hold values from -6 to 6
- grad_out: bfloat16 [2, 2048, 4096], P('dp', 'ctx'), may hold values from -6 to 6
- out_weight: bfloat16 [1024, 4096], P('ctx'), may hold values from -0.1875 to 0.1875
- short_taps: float32 [3, 1024, 7], replicated, may hold values from -2 to 2
- residues: float32 [1024, 16], replicated, may hold values from -1.5 to 1.5
- decay_rate: float32 [1024, 16], replicated, may hold values from 0.00012207031 to 0.05
Outputs:
- grad_query: bfloat16 [2, 2048, 1024], P('dp', 'ctx')
- grad_key: bfloat16 [2, 2048, 1024], P('dp', 'ctx')
- grad_value: bfloat16 [2, 2048, 1024], P('dp', 'ctx')
- weight_grad: float32 [1024, 4096], P('ctx')
- taps_grad: float32 [3, 1024, 7], replicated
- residue_grad: float32 [1024, 16], replicated
The draws below stay inside these ranges and needn't reach their ends.
All inputs are finite; a program needn't handle non-finite values.
Results may differ from the reference program's by a relative error of at most 0.0075.
Values may be sent and summed in bfloat16 or wider, within the bound.
A program may use at most 192 MiB of HBM per device.

```python
import math
import jax
import jax.numpy as jnp
from jax import lax

C = 1024
D = 4096
M = 16
L = 2048
BATCH = 2


def level_of(stream_key, extent, cuts, smallest, largest):
    def one(position, parts):
        heights = jax.random.uniform(jax.random.fold_in(jax.random.fold_in(stream_key, 6), position), (parts,), jnp.float32, smallest / len(cuts), largest / len(cuts))
        return jnp.repeat(jnp.exp(heights), extent[position] // parts).reshape((-1,) + (1,) * (len(extent) - position - 1))

    level = one(*cuts[0])
    for cut in cuts[1:]:
        level = level * one(*cut)
    return level


def noise(own_key, shape, spread, reach, pieces=(), dtype=jnp.bfloat16):
    values = jax.random.normal(own_key, shape, jnp.float32) * spread
    if len(pieces) > 0:
        values = level_of(own_key, shape, pieces, -0.22, 0.18) * values
    return jnp.clip(values, min=-reach, max=reach).astype(dtype)


def setup_inputs(seed: int = 0) -> dict:
    arg_keys = jax.random.split(jax.random.key(seed), 9)
    return {
        "query_proj": noise(arg_keys[0], (BATCH, L, C), 1.0, 6.0, ((0, 2), (1, 16))),
        "key_proj": noise(arg_keys[1], (BATCH, L, C), 1.0, 6.0, ((0, 2), (1, 16))),
        "value_proj": noise(arg_keys[2], (BATCH, L, C), 1.0, 6.0, ((0, 2), (1, 16))),
        "grad_out": noise(arg_keys[3], (BATCH, L, D), 1.0, 6.0, ((0, 2), (1, 16))),
        "out_weight": noise(arg_keys[4], (C, D), C ** -0.5, 0.1875, ((0, 16),)),
        "short_taps": noise(arg_keys[5], (3, C, 7), 7 ** -0.5, 2.0, (), jnp.float32),
        "residues": noise(arg_keys[6], (C, M), M ** -0.5, 1.5, (), jnp.float32),
        "decay_rate": jnp.clip(jnp.exp(jax.random.uniform(arg_keys[7], (C, M), jnp.float32, math.log(0.00012207031), math.log(0.05))), 0.00012207031, 0.05),
    }


def shift_sum(field, taps):
    length = field.shape[1]
    padded = jnp.pad(field, ((0, 0), (6, 0), (0, 0)))
    result = jnp.zeros_like(field)
    for lag in range(7):
        result = result + taps[:, lag] * padded[:, 6 - lag:6 - lag + length, :]
    return result

def adjoint_sum(grad, taps):
    length = grad.shape[1]
    padded = jnp.pad(grad, ((0, 0), (0, 6), (0, 0)))
    result = jnp.zeros_like(grad)
    for lag in range(7):
        result = result + taps[:, lag] * padded[:, lag:lag + length, :]
    return result

def tap_terms(grad, field):
    length = field.shape[1]
    padded = jnp.pad(field, ((0, 0), (6, 0), (0, 0)))
    return jnp.stack([lax.optimization_barrier(jnp.sum(grad * padded[:, 6 - lag:6 - lag + length, :], axis=(0, 1))) for lag in range(7)], axis=-1)

def reference(query_proj, key_proj, value_proj, grad_out, out_weight, short_taps, residues, decay_rate):
    query_f = query_proj.astype(jnp.float32)
    key_f = key_proj.astype(jnp.float32)
    value_f = value_proj.astype(jnp.float32)
    shaped_q = shift_sum(query_f, short_taps[0])
    shaped_k = shift_sum(key_f, short_taps[1])
    shaped_v = shift_sum(value_f, short_taps[2])
    mixed = shaped_k * shaped_v
    factor = jnp.exp(-decay_rate)
    norm = jnp.sqrt(-jnp.expm1(-2.0 * decay_rate))
    coef = residues * norm
    start = jnp.zeros((BATCH, C, M), jnp.float32)

    def forward_step(state, column):
        state = factor * state + column[:, :, None]
        return (state, lax.optimization_barrier(jnp.sum(coef * state, axis=-1)))
    _, filtered = lax.scan(forward_step, start, jnp.swapaxes(mixed, 0, 1))
    filtered = jnp.swapaxes(filtered, 0, 1)
    flat_out = grad_out.reshape(-1, D)
    upstream = jnp.dot(flat_out, out_weight.T, preferred_element_type=jnp.float32).reshape(BATCH, -1, C)
    gated = (shaped_q * filtered).astype(jnp.bfloat16)
    weight_grad = jnp.dot(gated.reshape(-1, C).T, flat_out, preferred_element_type=jnp.float32)
    grad_filtered = upstream * shaped_q
    grad_qs = upstream * filtered

    def backward_step(carry, columns):
        adjoint, total = carry
        grad_col, mix_col = columns
        adjoint = factor * adjoint + grad_col[:, :, None]
        total = total + mix_col[:, :, None] * adjoint
        return ((adjoint, total), lax.optimization_barrier(jnp.sum(coef * adjoint, axis=-1)))
    (_, total), grad_mixed = lax.scan(backward_step, (start, start), (jnp.swapaxes(grad_filtered, 0, 1), jnp.swapaxes(mixed, 0, 1)), reverse=True)
    grad_mixed = jnp.swapaxes(grad_mixed, 0, 1)
    residue_grad = norm * lax.optimization_barrier(jnp.sum(total, axis=0))
    grad_ks = grad_mixed * shaped_v
    grad_vs = grad_mixed * shaped_k
    grad_query = adjoint_sum(grad_qs, short_taps[0]).astype(jnp.bfloat16)
    grad_key = adjoint_sum(grad_ks, short_taps[1]).astype(jnp.bfloat16)
    grad_value = adjoint_sum(grad_vs, short_taps[2]).astype(jnp.bfloat16)
    taps_grad = jnp.stack([tap_terms(grad_qs, query_f), tap_terms(grad_ks, key_f), tap_terms(grad_vs, value_f)])
    return (grad_query, grad_key, grad_value, weight_grad, taps_grad, residue_grad)
```

```python
import functools
import math

import jax
import jax.numpy as jnp
from jax import lax
from jax.experimental import pallas as pl
from jax.experimental.pallas import tpu as pltpu
from jax.sharding import PartitionSpec as P

LANES = 128
CHUNKS = 8
HALO = 8
PIECES = 8
WPIECES = 4


def at_device(ctx, dp=None):
    return {"ctx": ctx} if dp is None else {"ctx": ctx, "dp": dp}


def greet_all(ctx_count, dp_count):
    barrier = pltpu.get_barrier_semaphore()
    me, row = lax.axis_index("ctx"), lax.axis_index("dp")
    for step in range(ctx_count):
        for other in range(dp_count):
            if step + other > 0:
                pl.semaphore_signal(
                    barrier,
                    inc=1,
                    device_id=at_device(
                        lax.rem(me + step, ctx_count),
                        None if dp_count == 1 else lax.rem(row + other, dp_count),
                    ),
                    device_id_type=pl.DeviceIdType.MESH,
                )
    return barrier


def remote(src, dst, send, recv, ctx, dp=None):
    return pltpu.make_async_remote_copy(
        src_ref=src,
        dst_ref=dst,
        send_sem=send,
        recv_sem=recv,
        device_id=at_device(ctx, dp),
        device_id_type=pl.DeviceIdType.MESH,
    )


def tree_sum(parts):
    parts = list(parts)
    while len(parts) > 1:
        parts = [
            parts[k] + parts[k + 1] if k + 1 < len(parts) else parts[k]
            for k in range(0, len(parts), 2)
        ]
    return parts[0]


def sums_first(j):
    return j % 3 == 2


def layer_kernel(group, count, rows_dp, names, *refs):
    r = dict(zip(names, refs))
    f32, bf16 = jnp.float32, jnp.bfloat16
    me, line = lax.axis_index("ctx"), lax.axis_index("dp")
    mine, block = lax.rem(me, group), lax.div(me, group)
    go_ref, w_ref = r["go"], r["w"]
    tokens, columns = go_ref.shape
    own_rows = w_ref.shape[0]
    width = count * own_rows
    modes = r["factor_in"].shape[0]
    span_tokens = group * tokens
    steps = span_tokens // CHUNKS
    chunk = columns // PIECES
    part = chunk // rows_dp
    wide = columns // WPIECES
    strip = wide // rows_dp
    members = count * rows_dp
    slot = block * rows_dp + line
    home = block * group
    across = lax.rem(mine + group // 2, group)
    twin = mine + 1 - 2 * lax.rem(mine, 2)
    spans = [slice(k, k + LANES) for k in range(0, width, LANES)]
    row = lax.broadcasted_iota(jnp.int32, (CHUNKS, LANES), 0)

    barrier = greet_all(group * count, rows_dp)

    def strands(ref, g, *lead):
        return jnp.concatenate(
            [
                ref[lead + (slice(None), pl.ds((k * group + g) * own_rows, own_rows))]
                for k in range(count)
            ],
            axis=1,
        )

    xs, xg, gog, wg = r["xs"], r["xg"], r["gog"], r["wg"]
    for i, name in enumerate(("q", "k", "v")):
        for g in range(group):
            xs[g, i] = strands(r[name], g)

    def picked(ref, *lead):
        value = strands(ref, 0, *lead)
        for g in range(1, group):
            value = jnp.where(mine == g, strands(ref, g, *lead), value)
        return value

    taps_ref, factor_ref, coef_ref = r["taps"], r["factor"], r["coef"]
    rate_row, norm_row = r["rate"], r["norm"]
    rate_row[...] = picked(r["rate_in"])
    norm_row[...] = picked(r["norm_in"])
    factor_rows, coef_rows = picked(r["factor_in"]), picked(r["coef_in"])
    for m in range(modes):
        factor_ref[m] = jnp.broadcast_to(factor_rows[m : m + 1], (CHUNKS, width))
        coef_ref[m] = jnp.broadcast_to(coef_rows[m : m + 1], (CHUNKS, width))
    for i in range(3):
        tap_rows = picked(r["taps_in"], i)
        for j in range(7):
            taps_ref[i, j] = jnp.broadcast_to(tap_rows[j : j + 1], (CHUNKS, width))

    pl.semaphore_wait(barrier, group * count * rows_dp - 1)

    streams = []
    for step in (2, 3, 1) if group == 4 else range(1, group):
        there = lax.rem(mine + step, group)
        streams.append(
            remote(xs.at[there], xg.at[mine], r["xsend"].at[step], r["xrecv"].at[step], home + there)
        )

    def halo_copy(there):
        ahead = jnp.minimum(block + 1, count - 1)
        return remote(
            xs.at[there, :, pl.ds(tokens - 16, 16), :],
            r["halo"],
            r["hsend"].at[there],
            r["hrecv"].at[0],
            ahead * group + there,
        )

    def token_rows(g):
        return pl.ds(pl.multiple_of(g * tokens, tokens), tokens)

    def weight_rows(b):
        return pl.ds(pl.multiple_of(b * own_rows, own_rows), own_rows)

    over, beside, passed = [], [], []
    for j in range(PIECES):
        cols = pl.ds(j * chunk, chunk)
        own = gog.at[token_rows(mine), cols]
        over.append(
            remote(go_ref.at[:, cols], own, r["gsend"].at[j], r["grecv"].at[j], home + across)
        )
        beside.append(
            remote(go_ref.at[:, cols], own, r["tsend"].at[j], r["trecv"].at[j], home + twin)
        )
        held = gog.at[token_rows(across), cols]
        passed.append(remote(held, held, r["fsend"].at[j], r["frecv"].at[j], home + twin))
    weights, swaps = [], []
    for p in range(WPIECES):
        cols = pl.ds(pl.multiple_of(p * wide + line * strip, strip), strip)
        weights.append([])
        swaps.append([])
        for step in range(1, count):
            at = p * count + step
            weights[p].append(
                remote(
                    w_ref.at[:, cols],
                    wg.at[weight_rows(block), cols],
                    r["wsend"].at[at],
                    r["wrecv"].at[at],
                    lax.rem(block + step, count) * group + mine,
                )
            )
            held = wg.at[weight_rows(lax.rem(block + count - step, count)), cols]
            for other in range(1, rows_dp):
                at = (p * count + step) * rows_dp + other
                to = lax.rem(line + other, rows_dp)
                swaps[p].append(
                    (step, remote(held, held, r["psend"].at[at], r["precv"].at[at], me, to))
                )

    def start(copies):
        for copy in copies:
            copy.start()

    start(streams)
    start(weights[0])
    start(over)

    @pl.when((mine == group - 1) & (block < count - 1))
    def _():
        for there in range(group):
            halo_copy(there).start()

    start(weights[1])
    start(beside)
    locals_ = [
        pltpu.make_async_copy(xs.at[mine], xg.at[mine], r["own"].at[0]),
        pltpu.make_async_copy(go_ref, gog.at[token_rows(mine)], r["own"].at[1]),
        pltpu.make_async_copy(w_ref, wg.at[weight_rows(block)], r["own"].at[2]),
    ]
    start(locals_)

    @pl.when(block == 0)
    def _():
        r["halo"][...] = jnp.zeros_like(r["halo"])

    def relay_weights(p):
        for step in range(1, count):
            weights[p][step - 1].wait_recv()
            for at, copy in swaps[p]:
                if at == step:
                    copy.start()

    def relay(j):
        over[j].wait_recv()
        passed[j].start()

    relay_weights(0)
    for copy in streams:
        copy.wait_recv()
    locals_[0].wait()

    @pl.when(block > 0)
    def _():
        halo_copy(0).wait_recv()

    def down(v):
        return jnp.where(row > 0, pltpu.roll(v, 1, 0), 0.0)

    def up(v):
        return jnp.where(row < CHUNKS - 1, pltpu.roll(v, CHUNKS - 1, 0), 0.0)

    x_ref, shaped, mixed, filtered_ref = r["x"], r["shaped"], r["mixed"], r["filtered"]
    gradf, gext, starts, bstarts = r["gradf"], r["gext"], r["starts"], r["bstarts"]
    fstates, bstates = r["fstates"], r["bstates"]
    zeros = tuple(jnp.zeros((CHUNKS, LANES), f32) for _ in range(modes))
    for span in spans:
        for i in range(3):
            value = xg[:, i, :, span].astype(f32).reshape(CHUNKS, steps, LANES)
            x_ref[i, HALO:, :, span] = jnp.swapaxes(value, 0, 1)
            before = r["halo"][i, :, span].astype(f32)
            for s in range(HALO):
                x_ref[i, s, :, span] = jnp.where(
                    row > 0,
                    pltpu.roll(x_ref[i, steps + s, :, span], 1, 0),
                    before[16 - HALO + s : 17 - HALO + s],
                )

        def first(s, state):
            made = []
            for i in range(3):
                total = tree_sum(
                    [taps_ref[i, j, :, span] * x_ref[i, s + HALO - j, :, span] for j in range(7)]
                )
                shaped[i, s, :, span] = total
                made.append(total)
            value = made[1] * made[2]
            mixed[s, :, span] = value
            return tuple(factor_ref[m, :, span] * state[m] + value for m in range(modes))

        ends = lax.fori_loop(0, steps, first, zeros)
        for m in range(modes):
            fs = jnp.broadcast_to(
                jnp.exp(-rate_row[m : m + 1, span] * float(steps)), (CHUNKS, LANES)
            )
            a = jnp.zeros((CHUNKS, LANES), f32)
            for _ in range(CHUNKS - 1):
                a = down(fs * a + ends[m])
            starts[m, :, span] = a
            fstates[block, m : m + 1, span] = (fs * a + ends[m])[CHUNKS - 1 :]

    def exchange(states, send, recv):
        return [
            remote(
                states.at[block],
                states.at[block],
                send.at[step],
                recv.at[step],
                lax.rem(block + step, count) * group + mine,
            )
            for step in range(1, count)
        ]

    forward = exchange(fstates, r["fssend"], r["fsrecv"])
    start(forward)
    for p in range(2, WPIECES):
        start(weights[p])

    acc = r["acc"]

    def upstream(j):
        if j == 0:
            locals_[1].wait()
            locals_[2].wait()
        if j * chunk % wide == 0:
            for _, copy in swaps[j * chunk // wide]:
                copy.wait_recv()
        beside[j].wait_recv()
        passed[j].wait_recv()
        cols = pl.ds(j * chunk, chunk)
        value = lax.dot_general(
            gog[:, cols], wg[:, cols], (((1,), (1,)), ((), ())), preferred_element_type=f32
        )
        acc[...] = value if j == 0 else acc[...] + value

    relay_weights(1)
    relay(0)
    relay(1)
    upstream(0)

    for copy in forward:
        copy.wait_recv()
    decay = jnp.exp(-rate_row[...] * float(steps * CHUNKS))
    place = row.astype(f32) * float(steps)
    incoming = jnp.zeros((modes, width), f32)
    for k in range(count):
        incoming = jnp.where(k < block, decay * incoming + fstates[k], incoming)

    gated_ref, gated_t = r["gated"], r["gated_t"]
    for n, span in enumerate(spans):
        for m in range(modes):
            rate = rate_row[m : m + 1, span]
            starts[m, :, span] += jnp.exp(-rate * place) * incoming[m : m + 1, span]

        def second(s, state):
            value = mixed[s, :, span]
            new = tuple(factor_ref[m, :, span] * state[m] + value for m in range(modes))
            filtered = tree_sum([coef_ref[m, :, span] * new[m] for m in range(modes)])
            filtered_ref[s, :, span] = filtered
            gated_ref[s, :, span] = shaped[0, s, :, span] * filtered
            return new

        lax.fori_loop(0, steps, second, tuple(starts[m, :, span] for m in range(modes)))
        gated_t[span, :] = jnp.swapaxes(
            jnp.swapaxes(gated_ref[:, :, span], 0, 1).reshape(span_tokens, LANES), 0, 1
        ).astype(bf16)
        if n == 0:
            relay(2)
    relay(3)

    wp, qbuf, qsum, qz, qpair = r["wp"], r["qbuf"], r["qsum"], r["qz"], r["qpair"]
    wbuf, pair, wg_out = r["wbuf"], r["pair"], r["wg_out"]

    def product(j):
        cols = pl.ds(j * chunk, chunk)
        value = jnp.dot(gated_t[...], gog[:, cols], preferred_element_type=f32).astype(bf16)
        for k in range(count):
            wp[k, :, cols] = value[k * own_rows : (k + 1) * own_rows]

    def to_block(step):
        return lax.rem(block + step, count)

    def to_line(step):
        return lax.rem(line + step, rows_dp)

    stages = []
    for j in range(PIECES):
        if sums_first(j):
            one = [
                remote(
                    wp.at[to_block(step), :, pl.ds(j * chunk, chunk)],
                    wbuf.at[j, step],
                    r["asend"].at[j * count + step],
                    r["arecv"].at[j * count + step],
                    to_block(step) * group + mine,
                )
                for step in range(1, count)
            ]
            two = [
                remote(
                    pair.at[j, line], pair.at[j, line],
                    r["bsend"].at[j * rows_dp + step], r["brecv"].at[j * rows_dp + step],
                    me, to_line(step),
                )
                for step in range(1, rows_dp)
            ]
            stages.append([one, two])
        else:
            one = [
                remote(
                    wp.at[
                        :, :, pl.ds(pl.multiple_of(j * chunk + to_line(step) * part, part), part)
                    ],
                    qbuf.at[j, step],
                    r["bsend"].at[j * rows_dp + step],
                    r["brecv"].at[j * rows_dp + step],
                    me,
                    to_line(step),
                )
                for step in range(1, rows_dp)
            ]
            two = [
                remote(
                    qsum.at[j, to_block(step)],
                    qz.at[j, step],
                    r["asend"].at[j * count + step],
                    r["arecv"].at[j * count + step],
                    to_block(step) * group + mine,
                )
                for step in range(1, count)
            ]
            three = [
                remote(
                    qpair.at[j, line], qpair.at[j, line],
                    r["csend"].at[j * rows_dp + step], r["crecv"].at[j * rows_dp + step],
                    me, to_line(step),
                )
                for step in range(1, rows_dp)
            ]
            stages.append([one, two, three])

    def reduce_one(j):
        product(j)
        start(stages[j][0])

    def reduce_two(j):
        for copy in stages[j][0]:
            copy.wait_recv()
        if sums_first(j):
            value = wp[block, :, pl.ds(j * chunk, chunk)].astype(f32)
            for step in range(1, count):
                value = value + wbuf[j, step].astype(f32)
            pair[j, line] = value.astype(bf16)
        else:
            source = pl.ds(pl.multiple_of(j * chunk + line * part, part), part)
            for k in range(count):
                value = wp[k, :, source].astype(f32)
                for step in range(1, rows_dp):
                    value = value + qbuf[j, step, k].astype(f32)
                qsum[j, k] = value.astype(bf16)
        start(stages[j][1])

    def reduce_three(j):
        for copy in stages[j][1]:
            copy.wait_recv()
        if sums_first(j):
            value = pair[j, 0].astype(f32)
            for other in range(1, rows_dp):
                value = value + pair[j, other].astype(f32)
            wg_out[:, pl.ds(j * chunk, chunk)] = value
        else:
            value = qsum[j, block].astype(f32)
            for step in range(1, count):
                value = value + qz[j, step].astype(f32)
            qpair[j, line] = value.astype(bf16)
            start(stages[j][2])

    def reduce_four(j):
        if not sums_first(j):
            for copy in stages[j][2]:
                copy.wait_recv()
            for other in range(rows_dp):
                wg_out[:, pl.ds(j * chunk + other * part, part)] = qpair[j, other].astype(f32)

    relay_weights(2)
    reduce_one(0)
    upstream(1)
    reduce_one(1)
    upstream(2)
    reduce_one(2)
    relay(4)
    upstream(3)
    reduce_one(3)
    relay_weights(3)
    relay(5)
    upstream(4)
    reduce_one(4)
    relay(6)
    upstream(5)
    reduce_one(5)
    relay(7)
    upstream(6)
    reduce_one(6)
    upstream(7)

    up_ref = r["up"]
    for span in spans:
        value = acc[:, span].reshape(CHUNKS, steps, LANES)
        up_ref[:, :, span] = jnp.swapaxes(value, 0, 1)

        def first_back(k, state):
            s = steps - 1 - k
            top = up_ref[s, :, span]
            gext[0, s, :, span] = top * filtered_ref[s, :, span]
            value = top * shaped[0, s, :, span]
            gradf[s, :, span] = value
            return tuple(factor_ref[m, :, span] * state[m] + value for m in range(modes))

        firsts = lax.fori_loop(0, steps, first_back, zeros)
        for m in range(modes):
            fs = jnp.broadcast_to(
                jnp.exp(-rate_row[m : m + 1, span] * float(steps)), (CHUNKS, LANES)
            )
            b = jnp.zeros((CHUNKS, LANES), f32)
            for _ in range(CHUNKS - 1):
                b = up(fs * b + firsts[m])
            bstarts[m, :, span] = b
            bstates[block, m : m + 1, span] = (fs * b + firsts[m])[:1]

    backward = exchange(bstates, r["bssend"], r["bsrecv"])
    start(backward)
    small_ref, edge, edge_in, y_ref = r["small"], r["edge"], r["edge_in"], r["y"]

    def edge_copy(first, size, at):
        return remote(
            edge.at[pl.ds(first, size)],
            edge_in.at[pl.ds(first, size)],
            r["esend"].at[at],
            r["erecv"].at[at],
            jnp.maximum(block - 1, 0) * group + mine,
        )

    def send_edge(first, size, at):
        for i in range(first, first + size):
            for s in range(HALO):
                edge[i, s : s + 1, :] = gext[i, s, 0:1, :]

        @pl.when(block > 0)
        def _():
            edge_copy(first, size, at).start()

    def take_edge(first, size, at):
        @pl.when(block == count - 1)
        def _():
            for i in range(first, first + size):
                edge_in[i] = jnp.zeros_like(edge_in[i])

        @pl.when(block < count - 1)
        def _():
            edge_copy(first, size, at).wait_recv()

    def tap_sums(i):
        for span in spans:

            def tap(s, sums):
                value = gext[i, s, :, span]
                return tuple(
                    sums[j] + value * x_ref[i, s + HALO - j, :, span] for j in range(7)
                )

            tapped = lax.fori_loop(0, steps, tap, zeros[:7], unroll=2)
            for j in range(7):
                at = i * 7 + j
                small_ref[at : at + 1, span] = jnp.sum(tapped[j], axis=0, keepdims=True)

    outs = []
    for i in range(3):
        outs.append([])
        for step in (2, 3, 1) if group == 4 else range(1, group):
            there = lax.rem(mine + step, group)
            at = i * group + step
            outs[i].append(
                remote(
                    y_ref.at[i, there], r["yo"].at[i, mine], r["ysend"].at[at], r["yrecv"].at[at],
                    home + there,
                )
            )
    keeps = [
        pltpu.make_async_copy(y_ref.at[i, mine], r["yo"].at[i, mine], r["own"].at[3 + i])
        for i in range(3)
    ]

    def send_out(i):
        for span in spans:
            for s in range(HALO):
                gext[i, steps + s, :, span] = jnp.where(
                    row < CHUNKS - 1,
                    pltpu.roll(gext[i, s, :, span], CHUNKS - 1, 0),
                    edge_in[i, s : s + 1, span],
                )

            def out(s, nothing):
                shaped[i, s, :, span] = tree_sum(
                    [taps_ref[i, j, :, span] * gext[i, s + j, :, span] for j in range(7)]
                )
                return nothing

            lax.fori_loop(0, steps, out, 0, unroll=2)
            value = jnp.swapaxes(shaped[i, :, :, span], 0, 1).astype(bf16)
            y_ref[i, :, :, span] = value.reshape(group, tokens, LANES)
        start(outs[i])
        keeps[i].start()

    send_edge(0, 1, 0)
    reduce_one(7)
    tap_sums(0)
    reduce_two(0)
    take_edge(0, 1, 0)
    send_out(0)
    for copy in backward:
        copy.wait_recv()
    outgoing = jnp.zeros((modes, width), f32)
    for k in range(count):
        other = count - 1 - k
        outgoing = jnp.where(other > block, decay * outgoing + bstates[other], outgoing)
    far = float(steps * (CHUNKS - 1)) - place
    for span in spans:
        for m in range(modes):
            rate = rate_row[m : m + 1, span]
            bstarts[m, :, span] += jnp.exp(-rate * far) * outgoing[m : m + 1, span]

        def second_back(k, carry):
            state, total = carry
            s = steps - 1 - k
            value = gradf[s, :, span]
            other = mixed[s, :, span]
            new = tuple(factor_ref[m, :, span] * state[m] + value for m in range(modes))
            total = tuple(total[m] + other * new[m] for m in range(modes))
            grad = tree_sum([coef_ref[m, :, span] * new[m] for m in range(modes)])
            gext[1, s, :, span] = grad * shaped[2, s, :, span]
            gext[2, s, :, span] = grad * shaped[1, s, :, span]
            return new, total

        _, total = lax.fori_loop(
            0, steps, second_back, (tuple(bstarts[m, :, span] for m in range(modes)), zeros)
        )
        for m in range(modes):
            small_ref[21 + m : 22 + m, span] = norm_row[m : m + 1, span] * jnp.sum(
                total[m], axis=0, keepdims=True
            )
    tall = small_ref.shape[0]
    if tall > 21 + modes:
        small_ref[21 + modes :, :] = jnp.zeros((tall - 21 - modes, width), f32)
    send_edge(1, 2, 1)
    tap_sums(1)
    tap_sums(2)

    sbuf, so = r["sbuf"], r["so"]
    smalls = []
    for step in range(1, members):
        there = lax.rem(slot + step, members)
        smalls.append(
            remote(
                small_ref,
                sbuf.at[slot],
                r["ssend"].at[step],
                r["srecv"].at[step],
                lax.div(there, rows_dp) * group + mine,
                lax.rem(there, rows_dp),
            )
        )
    totals = []
    for step in range(1, group):
        there = lax.rem(mine + step, group)
        totals.append(
            remote(so.at[mine], so.at[mine], r["osend"].at[step], r["orecv"].at[step], home + there)
        )
    sbuf[slot] = small_ref[...]
    start(smalls)
    take_edge(1, 2, 1)
    send_out(1)
    send_out(2)
    for j in range(1, PIECES):
        reduce_two(j)
    for copy in smalls:
        copy.wait_recv()
    total = sbuf[0]
    for k in range(1, members):
        total = total + sbuf[k]
    so[mine] = total
    start(totals)
    for j in range(PIECES):
        reduce_three(j)

    def joined(pieces):
        return jnp.concatenate(
            [
                pieces[g][:, k * own_rows : (k + 1) * own_rows]
                for k in range(count)
                for g in range(group)
            ],
            axis=1,
        )

    for i, name in enumerate(("gq_out", "gk_out", "gv_out")):
        for copy in outs[i]:
            copy.wait_recv()
        keeps[i].wait()
        r[name][...] = joined([r["yo"][i, g] for g in range(group)])
    for j in range(PIECES):
        reduce_four(j)
    for copy in totals:
        copy.wait_recv()
    sums = joined([so[g] for g in range(group)])
    for i in range(3):
        r["taps_out"][i] = sums[7 * i : 7 * i + 7]
    r["residue_out"][...] = sums[21 : 21 + modes]

    sent = streams + over + beside + passed + forward + backward + smalls + totals
    for copies in weights + outs + [copies for stage in stages for copies in stage]:
        sent = sent + copies
    for pieces in swaps:
        sent = sent + [copy for _, copy in pieces]
    for copy in sent:
        copy.wait_send()

    @pl.when((mine == group - 1) & (block < count - 1))
    def _():
        for there in range(group):
            halo_copy(there).wait_send()

    @pl.when(block > 0)
    def _():
        edge_copy(0, 1, 0).wait_send()
        edge_copy(1, 2, 1).wait_send()


VMEM = pl.BlockSpec(memory_space=pltpu.VMEM)
DMA = pltpu.SemaphoreType.DMA


def shards(
    query_proj, key_proj, value_proj, grad_out, out_weight, short_taps, residues, decay_rate
):
    devices, rows_dp = lax.axis_size("ctx"), lax.axis_size("dp")
    group = math.gcd(devices, 4)
    count = devices // group
    tokens, channels = query_proj.shape[1:]
    own_rows, columns = out_weight.shape
    width = count * own_rows
    modes = residues.shape[1]
    span_tokens = group * tokens
    steps = span_tokens // CHUNKS
    f32, bf16 = jnp.float32, jnp.bfloat16
    chunk = columns // PIECES
    part = chunk // rows_dp

    rate = decay_rate.T
    norm = jnp.sqrt(-jnp.expm1(-2.0 * rate))
    coef = residues.T * norm
    tall = (21 + modes + 7) // 8 * 8
    small = (tall, width)
    scan = (steps, CHUNKS, width)
    table = (modes, CHUNKS, width)
    scratch = {
        "xs": pltpu.VMEM((group, 3, tokens, width), bf16),
        "xg": pltpu.VMEM((group, 3, tokens, width), bf16),
        "gog": pltpu.VMEM((span_tokens, columns), bf16),
        "wg": pltpu.VMEM((width, columns), bf16),
        "halo": pltpu.VMEM((3, 16, width), bf16),
        "taps": pltpu.VMEM((3, 7, CHUNKS, width), f32),
        "factor": pltpu.VMEM(table, f32),
        "coef": pltpu.VMEM(table, f32),
        "rate": pltpu.VMEM((modes, width), f32),
        "norm": pltpu.VMEM((modes, width), f32),
        "x": pltpu.VMEM((3, steps + HALO, CHUNKS, width), f32),
        "shaped": pltpu.VMEM((3,) + scan, f32),
        "mixed": pltpu.VMEM(scan, f32),
        "filtered": pltpu.VMEM(scan, f32),
        "gated": pltpu.VMEM(scan, f32),
        "gradf": pltpu.VMEM(scan, f32),
        "up": pltpu.VMEM(scan, f32),
        "gext": pltpu.VMEM((3, steps + HALO, CHUNKS, width), f32),
        "starts": pltpu.VMEM(table, f32),
        "bstarts": pltpu.VMEM(table, f32),
        "fstates": pltpu.VMEM((count, modes, width), f32),
        "bstates": pltpu.VMEM((count, modes, width), f32),
        "acc": pltpu.VMEM((span_tokens, width), f32),
        "gated_t": pltpu.VMEM((width, span_tokens), bf16),
        "edge": pltpu.VMEM((3, HALO, width), f32),
        "edge_in": pltpu.VMEM((3, HALO, width), f32),
        "small": pltpu.VMEM(small, f32),
        "sbuf": pltpu.VMEM((count * rows_dp,) + small, f32),
        "so": pltpu.VMEM((group,) + small, f32),
        "y": pltpu.VMEM((3, group, tokens, width), bf16),
        "yo": pltpu.VMEM((3, group, tokens, width), bf16),
        "wp": pltpu.VMEM((count, own_rows, columns), bf16),
        "wbuf": pltpu.VMEM((PIECES, count, own_rows, chunk), bf16),
        "pair": pltpu.VMEM((PIECES, rows_dp, own_rows, chunk), bf16),
        "qbuf": pltpu.VMEM((PIECES, rows_dp, count, own_rows, part), bf16),
        "qsum": pltpu.VMEM((PIECES, count, own_rows, part), bf16),
        "qz": pltpu.VMEM((PIECES, count, own_rows, part), bf16),
        "qpair": pltpu.VMEM((PIECES, rows_dp, own_rows, part), bf16),
    }
    for name, size in (
        ("x", group), ("g", PIECES), ("t", PIECES), ("f", PIECES),
        ("w", WPIECES * count), ("p", WPIECES * count * rows_dp),
        ("fs", count), ("bs", count), ("e", 2),
        ("a", PIECES * count), ("b", PIECES * rows_dp), ("c", PIECES * rows_dp),
        ("s", count * rows_dp), ("o", group), ("y", 3 * group),
    ):
        scratch[name + "send"] = DMA((size,))
        scratch[name + "recv"] = DMA((size,))
    scratch.update(hsend=DMA((group,)), hrecv=DMA((1,)), own=DMA((6,)))
    ins = ("q", "k", "v", "go", "w", "taps_in", "factor_in", "coef_in", "rate_in", "norm_in")
    outs = ("gq_out", "gk_out", "gv_out", "wg_out", "taps_out", "residue_out")
    grads = jax.ShapeDtypeStruct((tokens, channels), bf16)
    gq, gk, gv, weight_grad, taps_grad, residue_grad = pl.pallas_call(
        functools.partial(layer_kernel, group, count, rows_dp, ins + outs + tuple(scratch)),
        out_shape=(
            grads,
            grads,
            grads,
            jax.ShapeDtypeStruct((own_rows, columns), f32),
            jax.ShapeDtypeStruct((3, 7, channels), f32),
            jax.ShapeDtypeStruct((modes, channels), f32),
        ),
        in_specs=[VMEM] * len(ins),
        out_specs=(VMEM,) * len(outs),
        scratch_shapes=list(scratch.values()),
        compiler_params=pltpu.CompilerParams(
            collective_id=0, has_side_effects=True, vmem_limit_bytes=60 * 1024 * 1024
        ),
        name="layer",
    )(
        query_proj[0], key_proj[0], value_proj[0], grad_out[0], out_weight,
        jnp.swapaxes(short_taps, 1, 2), jnp.exp(-rate), coef, rate, norm,
    )
    return (
        gq[None], gk[None], gv[None], weight_grad,
        jnp.swapaxes(taps_grad, 1, 2), residue_grad.T,
    )


def solution(mesh):
    placed = (
        P("dp", "ctx", None),
        P("dp", "ctx", None),
        P("dp", "ctx", None),
        P("dp", "ctx", None),
        P("ctx", None),
        P(),
        P(),
        P(),
    )
    return jax.shard_map(
        shards,
        mesh=mesh,
        in_specs=placed,
        out_specs=(
            P("dp", "ctx", None),
            P("dp", "ctx", None),
            P("dp", "ctx", None),
            P("ctx", None),
            P(),
            P(),
        ),
        check_vma=False,
    )
```

```python
import functools
import math

import jax
import jax.numpy as jnp
from jax import lax
from jax.experimental import pallas as pl
from jax.experimental.pallas import tpu as pltpu
from jax.sharding import PartitionSpec as P

LANES = 128
CHUNKS = 8
HALO = 8
PIECES = 8
WPIECES = 4


def at_device(ctx, dp=None):
    return {"ctx": ctx} if dp is None else {"ctx": ctx, "dp": dp}


def greet_all(ctx_count, dp_count):
    barrier = pltpu.get_barrier_semaphore()
    me, row = lax.axis_index("ctx"), lax.axis_index("dp")
    for step in range(ctx_count):
        for other in range(dp_count):
            if step + other > 0:
                pl.semaphore_signal(
                    barrier,
                    inc=1,
                    device_id=at_device(
                        lax.rem(me + step, ctx_count),
                        None if dp_count == 1 else lax.rem(row + other, dp_count),
                    ),
                    device_id_type=pl.DeviceIdType.MESH,
                )
    return barrier


def remote(src, dst, send, recv, ctx, dp=None):
    return pltpu.make_async_remote_copy(
        src_ref=src,
        dst_ref=dst,
        send_sem=send,
        recv_sem=recv,
        device_id=at_device(ctx, dp),
        device_id_type=pl.DeviceIdType.MESH,
    )


def tree_sum(parts):
    parts = list(parts)
    while len(parts) > 1:
        parts = [
            parts[k] + parts[k + 1] if k + 1 < len(parts) else parts[k]
            for k in range(0, len(parts), 2)
        ]
    return parts[0]


def sums_first(j):
    return j in (0, 3)


def layer_kernel(group, count, rows_dp, names, *refs):
    r = dict(zip(names, refs))
    f32, bf16 = jnp.float32, jnp.bfloat16
    me, line = lax.axis_index("ctx"), lax.axis_index("dp")
    mine, block = lax.rem(me, group), lax.div(me, group)
    go_ref, w_ref = r["go"], r["w"]
    tokens, columns = go_ref.shape
    own_rows = w_ref.shape[0]
    width = count * own_rows
    modes = r["factor_in"].shape[0]
    span_tokens = group * tokens
    steps = span_tokens // CHUNKS
    chunk = columns // PIECES
    part = chunk // rows_dp
    wide = columns // WPIECES
    strip = wide // rows_dp
    home = block * group
    across = lax.rem(mine + group // 2, group)
    twin = mine + 1 - 2 * lax.rem(mine, 2)
    spans = [slice(k, k + LANES) for k in range(0, width, LANES)]
    row = lax.broadcasted_iota(jnp.int32, (CHUNKS, LANES), 0)

    barrier = greet_all(group * count, rows_dp)

    def strands(ref, g, *lead):
        return jnp.concatenate(
            [
                ref[lead + (slice(None), pl.ds((k * group + g) * own_rows, own_rows))]
                for k in range(count)
            ],
            axis=1,
        )

    xs, xg, gog, wg = r["xs"], r["xg"], r["gog"], r["wg"]
    for i, name in enumerate(("q", "k", "v")):
        for g in range(group):
            xs[g, i] = strands(r[name], g)

    def picked(ref, *lead):
        value = strands(ref, 0, *lead)
        for g in range(1, group):
            value = jnp.where(mine == g, strands(ref, g, *lead), value)
        return value

    taps_ref, factor_ref, coef_ref = r["taps"], r["factor"], r["coef"]
    rate_row, norm_row = r["rate"], r["norm"]
    rate_row[...] = picked(r["rate_in"])
    norm_row[...] = picked(r["norm_in"])
    factor_rows, coef_rows = picked(r["factor_in"]), picked(r["coef_in"])
    for m in range(modes):
        factor_ref[m] = jnp.broadcast_to(factor_rows[m : m + 1], (CHUNKS, width))
        coef_ref[m] = jnp.broadcast_to(coef_rows[m : m + 1], (CHUNKS, width))
    for i in range(3):
        tap_rows = picked(r["taps_in"], i)
        for j in range(7):
            taps_ref[i, j] = jnp.broadcast_to(tap_rows[j : j + 1], (CHUNKS, width))

    pl.semaphore_wait(barrier, group * count * rows_dp - 1)

    streams = []
    for step in (2, 3, 1) if group == 4 else range(1, group):
        there = lax.rem(mine + step, group)
        streams.append(
            remote(xs.at[there], xg.at[mine], r["xsend"].at[step], r["xrecv"].at[step], home + there)
        )

    def halo_copy(there):
        ahead = jnp.minimum(block + 1, count - 1)
        return remote(
            xs.at[there, :, pl.ds(tokens - 16, 16), :],
            r["halo"],
            r["hsend"].at[there],
            r["hrecv"].at[0],
            ahead * group + there,
        )

    def token_rows(g):
        return pl.ds(pl.multiple_of(g * tokens, tokens), tokens)

    def weight_rows(b):
        return pl.ds(pl.multiple_of(b * own_rows, own_rows), own_rows)

    over, beside, passed = [], [], []
    for j in range(PIECES):
        cols = pl.ds(j * chunk, chunk)
        own = gog.at[token_rows(mine), cols]
        over.append(
            remote(go_ref.at[:, cols], own, r["gsend"].at[j], r["grecv"].at[j], home + across)
        )
        beside.append(
            remote(go_ref.at[:, cols], own, r["tsend"].at[j], r["trecv"].at[j], home + twin)
        )
        held = gog.at[token_rows(across), cols]
        passed.append(remote(held, held, r["fsend"].at[j], r["frecv"].at[j], home + twin))
    weights, swaps = [], []
    for p in range(WPIECES):
        cols = pl.ds(pl.multiple_of(p * wide + line * strip, strip), strip)
        weights.append([])
        swaps.append([])
        for step in range(1, count):
            at = p * count + step
            weights[p].append(
                remote(
                    w_ref.at[:, cols],
                    wg.at[weight_rows(block), cols],
                    r["wsend"].at[at],
                    r["wrecv"].at[at],
                    lax.rem(block + step, count) * group + mine,
                )
            )
            held = wg.at[weight_rows(lax.rem(block + count - step, count)), cols]
            for other in range(1, rows_dp):
                at = (p * count + step) * rows_dp + other
                to = lax.rem(line + other, rows_dp)
                swaps[p].append(
                    (step, remote(held, held, r["psend"].at[at], r["precv"].at[at], me, to))
                )

    def start(copies):
        for copy in copies:
            copy.start()

    start(streams)
    start(weights[0])
    start(over)

    @pl.when((mine == group - 1) & (block < count - 1))
    def _():
        for there in range(group):
            halo_copy(there).start()

    start(weights[1])
    start(beside)
    locals_ = [
        pltpu.make_async_copy(xs.at[mine], xg.at[mine], r["own"].at[0]),
        pltpu.make_async_copy(go_ref, gog.at[token_rows(mine)], r["own"].at[1]),
        pltpu.make_async_copy(w_ref, wg.at[weight_rows(block)], r["own"].at[2]),
    ]
    start(locals_)

    @pl.when(block == 0)
    def _():
        r["halo"][...] = jnp.zeros_like(r["halo"])

    def relay_weights(p):
        for step in range(1, count):
            weights[p][step - 1].wait_recv()
            for at, copy in swaps[p]:
                if at == step:
                    copy.start()

    def relay(j):
        over[j].wait_recv()
        passed[j].start()

    relay_weights(0)
    for copy in streams:
        copy.wait_recv()
    locals_[0].wait()

    @pl.when(block > 0)
    def _():
        halo_copy(0).wait_recv()

    def down(v):
        return jnp.where(row > 0, pltpu.roll(v, 1, 0), 0.0)

    def up(v):
        return jnp.where(row < CHUNKS - 1, pltpu.roll(v, CHUNKS - 1, 0), 0.0)

    x_ref, shaped, mixed, filtered_ref = r["x"], r["shaped"], r["mixed"], r["filtered"]
    gradf, gext, starts, bstarts = r["gradf"], r["gext"], r["starts"], r["bstarts"]
    fstates, bstates = r["fstates"], r["bstates"]
    zeros = tuple(jnp.zeros((CHUNKS, LANES), f32) for _ in range(modes))
    for span in spans:
        for i in range(3):
            value = xg[:, i, :, span].astype(f32).reshape(CHUNKS, steps, LANES)
            x_ref[i, HALO:, :, span] = jnp.swapaxes(value, 0, 1)
            before = r["halo"][i, :, span].astype(f32)
            for s in range(HALO):
                x_ref[i, s, :, span] = jnp.where(
                    row > 0,
                    pltpu.roll(x_ref[i, steps + s, :, span], 1, 0),
                    before[16 - HALO + s : 17 - HALO + s],
                )

        def first(s, state):
            made = []
            for i in range(3):
                total = tree_sum(
                    [taps_ref[i, j, :, span] * x_ref[i, s + HALO - j, :, span] for j in range(7)]
                )
                shaped[i, s, :, span] = total
                made.append(total)
            value = made[1] * made[2]
            mixed[s, :, span] = value
            return tuple(factor_ref[m, :, span] * state[m] + value for m in range(modes))

        ends = lax.fori_loop(0, steps, first, zeros)
        for m in range(modes):
            fs = jnp.broadcast_to(
                jnp.exp(-rate_row[m : m + 1, span] * float(steps)), (CHUNKS, LANES)
            )
            a = jnp.zeros((CHUNKS, LANES), f32)
            for _ in range(CHUNKS - 1):
                a = down(fs * a + ends[m])
            starts[m, :, span] = a
            fstates[block, m : m + 1, span] = (fs * a + ends[m])[CHUNKS - 1 :]

    def exchange(states, send, recv):
        return [
            remote(
                states.at[block],
                states.at[block],
                send.at[step],
                recv.at[step],
                lax.rem(block + step, count) * group + mine,
            )
            for step in range(1, count)
        ]

    forward = exchange(fstates, r["fssend"], r["fsrecv"])
    start(forward)
    for p in range(2, WPIECES):
        start(weights[p])

    acc = r["acc"]

    def upstream(j):
        if j == 0:
            locals_[1].wait()
            locals_[2].wait()
        if j * chunk % wide == 0:
            for _, copy in swaps[j * chunk // wide]:
                copy.wait_recv()
        beside[j].wait_recv()
        passed[j].wait_recv()
        cols = pl.ds(j * chunk, chunk)
        value = lax.dot_general(
            gog[:, cols], wg[:, cols], (((1,), (1,)), ((), ())), preferred_element_type=f32
        )
        acc[...] = value if j == 0 else acc[...] + value

    relay_weights(1)
    relay(0)
    relay(1)
    upstream(0)

    for copy in forward:
        copy.wait_recv()
    decay = jnp.exp(-rate_row[...] * float(steps * CHUNKS))
    place = row.astype(f32) * float(steps)
    incoming = jnp.zeros((modes, width), f32)
    for k in range(count):
        incoming = jnp.where(k < block, decay * incoming + fstates[k], incoming)

    gated_ref, gated_t = r["gated"], r["gated_t"]
    for n, span in enumerate(spans):
        for m in range(modes):
            rate = rate_row[m : m + 1, span]
            starts[m, :, span] += jnp.exp(-rate * place) * incoming[m : m + 1, span]

        def second(s, state):
            value = mixed[s, :, span]
            new = tuple(factor_ref[m, :, span] * state[m] + value for m in range(modes))
            filtered = tree_sum([coef_ref[m, :, span] * new[m] for m in range(modes)])
            filtered_ref[s, :, span] = filtered
            gated_ref[s, :, span] = shaped[0, s, :, span] * filtered
            return new

        lax.fori_loop(0, steps, second, tuple(starts[m, :, span] for m in range(modes)))
        gated_t[span, :] = jnp.swapaxes(
            jnp.swapaxes(gated_ref[:, :, span], 0, 1).reshape(span_tokens, LANES), 0, 1
        ).astype(bf16)
        if n == 0:
            relay(2)
    relay(3)

    wp, qbuf, qsum, qz, qpair = r["wp"], r["qbuf"], r["qsum"], r["qz"], r["qpair"]
    wbuf, pair, wg_out = r["wbuf"], r["pair"], r["wg_out"]

    def product(j):
        cols = pl.ds(j * chunk, chunk)
        value = jnp.dot(gated_t[...], gog[:, cols], preferred_element_type=f32).astype(bf16)
        for k in range(count):
            wp[k, :, cols] = value[k * own_rows : (k + 1) * own_rows]

    def to_block(step):
        return lax.rem(block + step, count)

    def to_line(step):
        return lax.rem(line + step, rows_dp)

    stages = []
    for j in range(PIECES):
        if sums_first(j):
            one = [
                remote(
                    wp.at[to_block(step), :, pl.ds(j * chunk, chunk)],
                    wbuf.at[j, step],
                    r["asend"].at[j * count + step],
                    r["arecv"].at[j * count + step],
                    to_block(step) * group + mine,
                )
                for step in range(1, count)
            ]
            two = [
                remote(
                    pair.at[j, line], pair.at[j, line],
                    r["bsend"].at[j * rows_dp + step], r["brecv"].at[j * rows_dp + step],
                    me, to_line(step),
                )
                for step in range(1, rows_dp)
            ]
            stages.append([one, two])
        else:
            one = [
                remote(
                    wp.at[
                        :, :, pl.ds(pl.multiple_of(j * chunk + to_line(step) * part, part), part)
                    ],
                    qbuf.at[j, step],
                    r["bsend"].at[j * rows_dp + step],
                    r["brecv"].at[j * rows_dp + step],
                    me,
                    to_line(step),
                )
                for step in range(1, rows_dp)
            ]
            two = [
                remote(
                    qsum.at[j, to_block(step)],
                    qz.at[j, step],
                    r["asend"].at[j * count + step],
                    r["arecv"].at[j * count + step],
                    to_block(step) * group + mine,
                )
                for step in range(1, count)
            ]
            three = [
                remote(
                    qpair.at[j, line], qpair.at[j, line],
                    r["csend"].at[j * rows_dp + step], r["crecv"].at[j * rows_dp + step],
                    me, to_line(step),
                )
                for step in range(1, rows_dp)
            ]
            stages.append([one, two, three])

    def reduce_one(j):
        product(j)
        start(stages[j][0])

    def reduce_two(j):
        for copy in stages[j][0]:
            copy.wait_recv()
        if sums_first(j):
            value = wp[block, :, pl.ds(j * chunk, chunk)].astype(f32)
            for step in range(1, count):
                value = value + wbuf[j, step].astype(f32)
            pair[j, line] = value.astype(bf16)
        else:
            source = pl.ds(pl.multiple_of(j * chunk + line * part, part), part)
            for k in range(count):
                value = wp[k, :, source].astype(f32)
                for step in range(1, rows_dp):
                    value = value + qbuf[j, step, k].astype(f32)
                qsum[j, k] = value.astype(bf16)
        start(stages[j][1])

    def reduce_three(j):
        for copy in stages[j][1]:
            copy.wait_recv()
        if sums_first(j):
            value = pair[j, 0].astype(f32)
            for other in range(1, rows_dp):
                value = value + pair[j, other].astype(f32)
            wg_out[:, pl.ds(j * chunk, chunk)] = value
        else:
            value = qsum[j, block].astype(f32)
            for step in range(1, count):
                value = value + qz[j, step].astype(f32)
            qpair[j, line] = value.astype(bf16)
            start(stages[j][2])

    def reduce_four(j):
        if not sums_first(j):
            for copy in stages[j][2]:
                copy.wait_recv()
            for other in range(rows_dp):
                wg_out[:, pl.ds(j * chunk + other * part, part)] = qpair[j, other].astype(f32)

    relay_weights(2)
    reduce_one(0)
    upstream(1)
    upstream(2)
    relay(4)
    upstream(3)
    reduce_one(3)
    relay_weights(3)
    reduce_one(1)
    relay(5)
    reduce_one(2)
    upstream(4)
    relay(6)
    reduce_one(4)
    upstream(5)
    reduce_one(5)
    relay(7)
    upstream(6)
    upstream(7)

    up_ref = r["up"]
    for span in spans:
        value = acc[:, span].reshape(CHUNKS, steps, LANES)
        up_ref[:, :, span] = jnp.swapaxes(value, 0, 1)

        def first_back(k, state):
            s = steps - 1 - k
            top = up_ref[s, :, span]
            gext[0, s, :, span] = top * filtered_ref[s, :, span]
            value = top * shaped[0, s, :, span]
            gradf[s, :, span] = value
            return tuple(factor_ref[m, :, span] * state[m] + value for m in range(modes))

        firsts = lax.fori_loop(0, steps, first_back, zeros)
        for m in range(modes):
            fs = jnp.broadcast_to(
                jnp.exp(-rate_row[m : m + 1, span] * float(steps)), (CHUNKS, LANES)
            )
            b = jnp.zeros((CHUNKS, LANES), f32)
            for _ in range(CHUNKS - 1):
                b = up(fs * b + firsts[m])
            bstarts[m, :, span] = b
            bstates[block, m : m + 1, span] = (fs * b + firsts[m])[:1]

    backward = exchange(bstates, r["bssend"], r["bsrecv"])
    start(backward)
    small_ref, edge, edge_in, y_ref = r["small"], r["edge"], r["edge_in"], r["y"]

    def edge_copy(first, size, at):
        return remote(
            edge.at[pl.ds(first, size)],
            edge_in.at[pl.ds(first, size)],
            r["esend"].at[at],
            r["erecv"].at[at],
            jnp.maximum(block - 1, 0) * group + mine,
        )

    def send_edge(first, size, at):
        for i in range(first, first + size):
            for s in range(HALO):
                edge[i, s : s + 1, :] = gext[i, s, 0:1, :]

        @pl.when(block > 0)
        def _():
            edge_copy(first, size, at).start()

    def take_edge(first, size, at):
        @pl.when(block == count - 1)
        def _():
            for i in range(first, first + size):
                edge_in[i] = jnp.zeros_like(edge_in[i])

        @pl.when(block < count - 1)
        def _():
            edge_copy(first, size, at).wait_recv()

    def tap_sums(i):
        for span in spans:

            def tap(s, sums):
                value = gext[i, s, :, span]
                return tuple(
                    sums[j] + value * x_ref[i, s + HALO - j, :, span] for j in range(7)
                )

            tapped = lax.fori_loop(0, steps, tap, zeros[:7], unroll=2)
            for j in range(7):
                at = i * 7 + j
                small_ref[at : at + 1, span] = jnp.sum(tapped[j], axis=0, keepdims=True)

    outs = []
    for i in range(3):
        outs.append([])
        for step in (2, 3, 1) if group == 4 else range(1, group):
            there = lax.rem(mine + step, group)
            at = i * group + step
            outs[i].append(
                remote(
                    y_ref.at[i, there], r["yo"].at[i, mine], r["ysend"].at[at], r["yrecv"].at[at],
                    home + there,
                )
            )
    keeps = [
        pltpu.make_async_copy(y_ref.at[i, mine], r["yo"].at[i, mine], r["own"].at[3 + i])
        for i in range(3)
    ]

    def send_out(i):
        for span in spans:
            for s in range(HALO):
                gext[i, steps + s, :, span] = jnp.where(
                    row < CHUNKS - 1,
                    pltpu.roll(gext[i, s, :, span], CHUNKS - 1, 0),
                    edge_in[i, s : s + 1, span],
                )

            def out(s, nothing):
                shaped[i, s, :, span] = tree_sum(
                    [taps_ref[i, j, :, span] * gext[i, s + j, :, span] for j in range(7)]
                )
                return nothing

            lax.fori_loop(0, steps, out, 0, unroll=2)
            value = jnp.swapaxes(shaped[i, :, :, span], 0, 1).astype(bf16)
            y_ref[i, :, :, span] = value.reshape(group, tokens, LANES)
        start(outs[i])
        keeps[i].start()

    send_edge(0, 1, 0)
    reduce_one(6)
    reduce_one(7)
    reduce_two(0)
    tap_sums(0)
    reduce_two(1)
    take_edge(0, 1, 0)
    send_out(0)
    reduce_two(2)
    for copy in backward:
        copy.wait_recv()
    outgoing = jnp.zeros((modes, width), f32)
    for k in range(count):
        other = count - 1 - k
        outgoing = jnp.where(other > block, decay * outgoing + bstates[other], outgoing)
    far = float(steps * (CHUNKS - 1)) - place
    for span in spans:
        for m in range(modes):
            rate = rate_row[m : m + 1, span]
            bstarts[m, :, span] += jnp.exp(-rate * far) * outgoing[m : m + 1, span]

        def second_back(k, carry):
            state, total = carry
            s = steps - 1 - k
            value = gradf[s, :, span]
            other = mixed[s, :, span]
            new = tuple(factor_ref[m, :, span] * state[m] + value for m in range(modes))
            total = tuple(total[m] + other * new[m] for m in range(modes))
            grad = tree_sum([coef_ref[m, :, span] * new[m] for m in range(modes)])
            gext[1, s, :, span] = grad * shaped[2, s, :, span]
            gext[2, s, :, span] = grad * shaped[1, s, :, span]
            return new, total

        _, total = lax.fori_loop(
            0, steps, second_back, (tuple(bstarts[m, :, span] for m in range(modes)), zeros)
        )
        for m in range(modes):
            small_ref[21 + m : 22 + m, span] = norm_row[m : m + 1, span] * jnp.sum(
                total[m], axis=0, keepdims=True
            )
    tall = small_ref.shape[0]
    if tall > 21 + modes:
        small_ref[21 + modes :, :] = jnp.zeros((tall - 21 - modes, width), f32)
    send_edge(1, 2, 1)
    reduce_two(3)
    reduce_two(4)
    tap_sums(1)
    tap_sums(2)

    sbuf, rsum, rbuf, so = r["sbuf"], r["rsum"], r["rbuf"], r["so"]
    smalls = [
        remote(
            small_ref, sbuf.at[step], r["ssend"].at[step], r["srecv"].at[step], me, to_line(step)
        )
        for step in range(1, rows_dp)
    ]
    rows = [
        remote(
            rsum, rbuf.at[step], r["rsend"].at[step], r["rrecv"].at[step],
            to_block(step) * group + mine,
        )
        for step in range(1, count)
    ]
    totals = []
    for step in range(1, group):
        there = lax.rem(mine + step, group)
        totals.append(
            remote(so.at[mine], so.at[mine], r["osend"].at[step], r["orecv"].at[step], home + there)
        )
    start(smalls)
    reduce_two(5)
    take_edge(1, 2, 1)
    send_out(1)
    for copy in smalls:
        copy.wait_recv()
    total = small_ref[...]
    for step in range(1, rows_dp):
        total = total + sbuf[step]
    rsum[...] = total
    start(rows)
    send_out(2)
    reduce_two(6)
    reduce_two(7)
    reduce_three(0)
    for copy in rows:
        copy.wait_recv()
    total = rsum[...]
    for step in range(1, count):
        total = total + rbuf[step]
    so[mine] = total
    start(totals)
    for j in range(1, PIECES):
        reduce_three(j)

    def joined(pieces):
        return jnp.concatenate(
            [
                pieces[g][:, k * own_rows : (k + 1) * own_rows]
                for k in range(count)
                for g in range(group)
            ],
            axis=1,
        )

    for i, name in enumerate(("gq_out", "gk_out", "gv_out")):
        for copy in outs[i]:
            copy.wait_recv()
        keeps[i].wait()
        r[name][...] = joined([r["yo"][i, g] for g in range(group)])
    for j in range(PIECES):
        reduce_four(j)
    for copy in totals:
        copy.wait_recv()
    sums = joined([so[g] for g in range(group)])
    for i in range(3):
        r["taps_out"][i] = sums[7 * i : 7 * i + 7]
    r["residue_out"][...] = sums[21 : 21 + modes]

    sent = streams + over + beside + passed + forward + backward + smalls + rows + totals
    for copies in weights + outs + [copies for stage in stages for copies in stage]:
        sent = sent + copies
    for pieces in swaps:
        sent = sent + [copy for _, copy in pieces]
    for copy in sent:
        copy.wait_send()

    @pl.when((mine == group - 1) & (block < count - 1))
    def _():
        for there in range(group):
            halo_copy(there).wait_send()

    @pl.when(block > 0)
    def _():
        edge_copy(0, 1, 0).wait_send()
        edge_copy(1, 2, 1).wait_send()


def finish_kernel(*refs):
    half = len(refs) // 2
    done = refs[-1]
    copies = [
        pltpu.make_async_copy(src, dst, done.at[k])
        for k, (src, dst) in enumerate(zip(refs[:half], refs[half:-1]))
    ]
    for copy in copies:
        copy.start()
    for copy in copies:
        copy.wait()


VMEM = pl.BlockSpec(memory_space=pltpu.VMEM)
ANY = pl.BlockSpec(memory_space=pl.ANY)
DMA = pltpu.SemaphoreType.DMA


def shards(
    query_proj, key_proj, value_proj, grad_out, out_weight, short_taps, residues, decay_rate
):
    devices, rows_dp = lax.axis_size("ctx"), lax.axis_size("dp")
    group = math.gcd(devices, 4)
    count = devices // group
    tokens, channels = query_proj.shape[1:]
    own_rows, columns = out_weight.shape
    width = count * own_rows
    modes = residues.shape[1]
    span_tokens = group * tokens
    steps = span_tokens // CHUNKS
    f32, bf16 = jnp.float32, jnp.bfloat16
    chunk = columns // PIECES
    part = chunk // rows_dp

    rate = decay_rate.T
    norm = jnp.sqrt(-jnp.expm1(-2.0 * rate))
    coef = residues.T * norm
    tall = (21 + modes + 7) // 8 * 8
    small = (tall, width)
    scan = (steps, CHUNKS, width)
    table = (modes, CHUNKS, width)
    scratch = {
        "xs": pltpu.VMEM((group, 3, tokens, width), bf16),
        "xg": pltpu.VMEM((group, 3, tokens, width), bf16),
        "gog": pltpu.VMEM((span_tokens, columns), bf16),
        "wg": pltpu.VMEM((width, columns), bf16),
        "halo": pltpu.VMEM((3, 16, width), bf16),
        "taps": pltpu.VMEM((3, 7, CHUNKS, width), f32),
        "factor": pltpu.VMEM(table, f32),
        "coef": pltpu.VMEM(table, f32),
        "rate": pltpu.VMEM((modes, width), f32),
        "norm": pltpu.VMEM((modes, width), f32),
        "x": pltpu.VMEM((3, steps + HALO, CHUNKS, width), f32),
        "shaped": pltpu.VMEM((3,) + scan, f32),
        "mixed": pltpu.VMEM(scan, f32),
        "filtered": pltpu.VMEM(scan, f32),
        "gated": pltpu.VMEM(scan, f32),
        "gradf": pltpu.VMEM(scan, f32),
        "up": pltpu.VMEM(scan, f32),
        "gext": pltpu.VMEM((3, steps + HALO, CHUNKS, width), f32),
        "starts": pltpu.VMEM(table, f32),
        "bstarts": pltpu.VMEM(table, f32),
        "fstates": pltpu.VMEM((count, modes, width), f32),
        "bstates": pltpu.VMEM((count, modes, width), f32),
        "acc": pltpu.VMEM((span_tokens, width), f32),
        "gated_t": pltpu.VMEM((width, span_tokens), bf16),
        "edge": pltpu.VMEM((3, HALO, width), f32),
        "edge_in": pltpu.VMEM((3, HALO, width), f32),
        "small": pltpu.VMEM(small, f32),
        "sbuf": pltpu.VMEM((rows_dp,) + small, f32),
        "rsum": pltpu.VMEM(small, f32),
        "rbuf": pltpu.VMEM((count,) + small, f32),
        "so": pltpu.VMEM((group,) + small, f32),
        "y": pltpu.VMEM((3, group, tokens, width), bf16),
        "yo": pltpu.VMEM((3, group, tokens, width), bf16),
        "wp": pltpu.VMEM((count, own_rows, columns), bf16),
        "wbuf": pltpu.VMEM((PIECES, count, own_rows, chunk), bf16),
        "pair": pltpu.VMEM((PIECES, rows_dp, own_rows, chunk), bf16),
        "qbuf": pltpu.VMEM((PIECES, rows_dp, count, own_rows, part), bf16),
        "qsum": pltpu.VMEM((PIECES, count, own_rows, part), bf16),
        "qz": pltpu.VMEM((PIECES, count, own_rows, part), bf16),
        "qpair": pltpu.VMEM((PIECES, rows_dp, own_rows, part), bf16),
    }
    for name, size in (
        ("x", group), ("g", PIECES), ("t", PIECES), ("f", PIECES),
        ("w", WPIECES * count), ("p", WPIECES * count * rows_dp),
        ("fs", count), ("bs", count), ("e", 2),
        ("a", PIECES * count), ("b", PIECES * rows_dp), ("c", PIECES * rows_dp),
        ("s", rows_dp), ("r", count), ("o", group), ("y", 3 * group),
    ):
        scratch[name + "send"] = DMA((size,))
        scratch[name + "recv"] = DMA((size,))
    scratch.update(hsend=DMA((group,)), hrecv=DMA((1,)), own=DMA((6,)))
    ins = ("q", "k", "v", "go", "w", "taps_in", "factor_in", "coef_in", "rate_in", "norm_in")
    outs = ("gq_out", "gk_out", "gv_out", "wg_out", "taps_out", "residue_out")
    grads = jax.ShapeDtypeStruct((tokens, channels), bf16)
    results = (
        grads,
        grads,
        grads,
        jax.ShapeDtypeStruct((own_rows, columns), f32),
        jax.ShapeDtypeStruct((3, 7, channels), f32),
        jax.ShapeDtypeStruct((modes, channels), f32),
    )
    made = pl.pallas_call(
        functools.partial(layer_kernel, group, count, rows_dp, ins + outs + tuple(scratch)),
        out_shape=results,
        in_specs=[VMEM] * len(ins),
        out_specs=(VMEM,) * len(outs),
        scratch_shapes=list(scratch.values()),
        compiler_params=pltpu.CompilerParams(
            collective_id=0, has_side_effects=True, vmem_limit_bytes=48 * 1024 * 1024
        ),
        name="layer",
    )(
        query_proj[0], key_proj[0], value_proj[0], grad_out[0], out_weight,
        jnp.swapaxes(short_taps, 1, 2), jnp.exp(-rate), coef, rate, norm,
    )
    gq, gk, gv, weight_grad, taps_grad, residue_grad = pl.pallas_call(
        finish_kernel,
        out_shape=results,
        in_specs=[ANY] * len(outs),
        out_specs=(ANY,) * len(outs),
        scratch_shapes=[DMA((len(outs),))],
        compiler_params=pltpu.CompilerParams(vmem_limit_bytes=4 * 1024 * 1024),
        name="finish",
    )(*made)
    return (
        gq[None], gk[None], gv[None], weight_grad,
        jnp.swapaxes(taps_grad, 1, 2), residue_grad.T,
    )


def solution(mesh):
    placed = (
        P("dp", "ctx", None),
        P("dp", "ctx", None),
        P("dp", "ctx", None),
        P("dp", "ctx", None),
        P("ctx", None),
        P(),
        P(),
        P(),
    )
    return jax.shard_map(
        shards,
        mesh=mesh,
        in_specs=placed,
        out_specs=(
            P("dp", "ctx", None),
            P("dp", "ctx", None),
            P("dp", "ctx", None),
            P("ctx", None),
            P(),
            P(),
        ),
        check_vma=False,
    )
```

```python
import functools
import math

import jax
import jax.numpy as jnp
from jax import lax
from jax.experimental import pallas as pl
from jax.experimental.pallas import tpu as pltpu
from jax.sharding import PartitionSpec as P

LANES = 128
CHUNKS = 8
HALO = 8
PIECES = 8
WPIECES = 4
TABLES = ("q", "k", "v", "taps", "factor", "coef", "rate", "norm")


def at_device(ctx, dp=None):
    return {"ctx": ctx} if dp is None else {"ctx": ctx, "dp": dp}


def greet_all(ctx_count, dp_count):
    barrier = pltpu.get_barrier_semaphore()
    me, row = lax.axis_index("ctx"), lax.axis_index("dp")
    for step in range(ctx_count):
        for other in range(dp_count):
            if step + other > 0:
                pl.semaphore_signal(
                    barrier,
                    inc=1,
                    device_id=at_device(
                        lax.rem(me + step, ctx_count),
                        None if dp_count == 1 else lax.rem(row + other, dp_count),
                    ),
                    device_id_type=pl.DeviceIdType.MESH,
                )
    return barrier


def remote(src, dst, send, recv, ctx, dp=None):
    return pltpu.make_async_remote_copy(
        src_ref=src,
        dst_ref=dst,
        send_sem=send,
        recv_sem=recv,
        device_id=at_device(ctx, dp),
        device_id_type=pl.DeviceIdType.MESH,
    )


def drain(view, sem):
    pltpu.make_async_copy(view, view, sem).wait()


def tree_sum(parts):
    parts = list(parts)
    while len(parts) > 1:
        parts = [
            parts[k] + parts[k + 1] if k + 1 < len(parts) else parts[k]
            for k in range(0, len(parts), 2)
        ]
    return parts[0]


def sums_first(j):
    return j == 0


def layer_kernel(group, count, rows_dp, names, *refs):
    r = dict(zip(names, refs))
    f32, bf16 = jnp.float32, jnp.bfloat16
    me, line = lax.axis_index("ctx"), lax.axis_index("dp")
    mine, block = lax.rem(me, group), lax.div(me, group)
    go_ref, w_ref = r["go_in"], r["w_in"]
    tokens, columns = go_ref.shape
    own_rows = w_ref.shape[0]
    width = count * own_rows
    modes = r["factor"].shape[0]
    span_tokens = group * tokens
    steps = span_tokens // CHUNKS
    chunk = columns // PIECES
    part = chunk // rows_dp
    wide = columns // WPIECES
    strip = wide // rows_dp
    home = block * group
    across = lax.rem(mine + group // 2, group)
    twin = mine + 1 - 2 * lax.rem(mine, 2)
    spans = [slice(k, k + LANES) for k in range(0, width, LANES)]
    row = lax.broadcasted_iota(jnp.int32, (CHUNKS, LANES), 0)

    def token_rows(g):
        return pl.ds(pl.multiple_of(g * tokens, tokens), tokens)

    def weight_rows(b):
        return pl.ds(pl.multiple_of(b * own_rows, own_rows), own_rows)

    xs, xg, gog, wg = r["xs"], r["xg"], r["gog"], r["wg"]
    go_own, w_own = gog.at[token_rows(mine)], wg.at[weight_rows(block)]
    loads = {
        name: pltpu.make_async_copy(r[name + "_in"], r[name], r["load"].at[k])
        for k, name in enumerate(TABLES)
    }
    loads["w"] = pltpu.make_async_copy(w_ref, w_own, r["load"].at[len(TABLES)])
    loads["go"] = pltpu.make_async_copy(go_ref, go_own, r["load"].at[len(TABLES) + 1])
    for copy in loads.values():
        copy.start()
    barrier = greet_all(group * count, rows_dp)

    def strands(ref, g, *lead):
        return jnp.concatenate(
            [
                ref[lead + (slice(None), pl.ds((k * group + g) * own_rows, own_rows))]
                for k in range(count)
            ],
            axis=1,
        )

    for name in TABLES:
        loads[name].wait()
    for i, name in enumerate(("q", "k", "v")):
        for g in range(group):
            xs[g, i] = strands(r[name], g)

    def picked(ref, *lead):
        value = strands(ref, 0, *lead)
        for g in range(1, group):
            value = jnp.where(mine == g, strands(ref, g, *lead), value)
        return value

    taps_ref, factor_ref, coef_ref = r["tap_tiles"], r["factor_tiles"], r["coef_tiles"]
    rate_row, norm_row = r["rate_rows"], r["norm_rows"]
    rate_row[...] = picked(r["rate"])
    norm_row[...] = picked(r["norm"])
    factor_rows, coef_rows = picked(r["factor"]), picked(r["coef"])
    for m in range(modes):
        factor_ref[m] = jnp.broadcast_to(factor_rows[m : m + 1], (CHUNKS, width))
        coef_ref[m] = jnp.broadcast_to(coef_rows[m : m + 1], (CHUNKS, width))
    for i in range(3):
        tap_rows = picked(r["taps"], i)
        for j in range(7):
            taps_ref[i, j] = jnp.broadcast_to(tap_rows[j : j + 1], (CHUNKS, width))

    loads["w"].wait()
    loads["go"].wait()
    pl.semaphore_wait(barrier, group * count * rows_dp - 1)

    streams = []
    for step in (2, 3, 1) if group == 4 else range(1, group):
        there = lax.rem(mine + step, group)
        streams.append(
            remote(xs.at[there], xg.at[mine], r["xsend"].at[0], r["xrecv"].at[0], home + there)
        )

    def halo_copy(there):
        ahead = jnp.minimum(block + 1, count - 1)
        return remote(
            xs.at[there, :, pl.ds(tokens - 16, 16), :],
            r["halo"],
            r["hsend"].at[0],
            r["hrecv"].at[0],
            ahead * group + there,
        )

    over, beside, passed = [], [], []
    for j in range(PIECES):
        cols = pl.ds(j * chunk, chunk)
        own = gog.at[token_rows(mine), cols]
        over.append(
            remote(own, own, r["gsend"].at[0], r["grecv"].at[j], home + across)
        )
        beside.append(
            remote(own, own, r["tsend"].at[0], r["trecv"].at[j], home + twin)
        )
        held = gog.at[token_rows(across), cols]
        passed.append(remote(held, held, r["fsend"].at[0], r["trecv"].at[j], home + twin))
    weights, swaps = [], []
    for p in range(WPIECES):
        cols = pl.ds(pl.multiple_of(p * wide + line * strip, strip), strip)
        weights.append([])
        swaps.append([])
        for step in range(1, count):
            at = p * (count - 1) + step - 1
            weights[p].append(
                remote(
                    wg.at[weight_rows(block), cols],
                    wg.at[weight_rows(block), cols],
                    r["wsend"].at[0],
                    r["wrecv"].at[at],
                    lax.rem(block + step, count) * group + mine,
                )
            )
            held = wg.at[weight_rows(lax.rem(block + count - step, count)), cols]
            for other in range(1, rows_dp):
                to = lax.rem(line + other, rows_dp)
                swaps[p].append(
                    (step, remote(held, held, r["psend"].at[0], r["precv"].at[p], me, to))
                )

    def start(copies):
        for copy in copies:
            copy.start()

    start(streams)
    start(weights[0])
    start(over)

    @pl.when((mine == group - 1) & (block < count - 1))
    def _():
        for there in range(group):
            halo_copy(there).start()

    start(weights[1])
    start(weights[2])
    start(beside)
    xs_own = pltpu.make_async_copy(xs.at[mine], xg.at[mine], r["own"].at[0])
    xs_own.start()

    @pl.when(block == 0)
    def _():
        r["halo"][...] = jnp.zeros_like(r["halo"])

    def relay_weights(p):
        for step in range(1, count):
            weights[p][step - 1].wait_recv()
            for at, copy in swaps[p]:
                if at == step:
                    copy.start()

    def relay(j):
        over[j].wait_recv()
        passed[j].start()

    relay_weights(0)
    drain(xg.at[pl.ds(0, group - 1)], r["xrecv"].at[0])
    xs_own.wait()

    @pl.when(block > 0)
    def _():
        halo_copy(0).wait_recv()

    def down(v):
        return jnp.where(row > 0, pltpu.roll(v, 1, 0), 0.0)

    def up(v):
        return jnp.where(row < CHUNKS - 1, pltpu.roll(v, CHUNKS - 1, 0), 0.0)

    x_ref, shaped, mixed, filtered_ref = r["x"], r["shaped"], r["mixed"], r["filtered"]
    gradf, gext, starts, bstarts = r["gradf"], r["gext"], r["starts"], r["bstarts"]
    fstates, bstates = r["fstates"], r["bstates"]
    zeros = tuple(jnp.zeros((CHUNKS, LANES), f32) for _ in range(modes))
    for span in spans:
        for i in range(3):
            value = xg[:, i, :, span].astype(f32).reshape(CHUNKS, steps, LANES)
            x_ref[i, HALO:, :, span] = jnp.swapaxes(value, 0, 1)
            before = r["halo"][i, :, span].astype(f32)
            for s in range(HALO):
                x_ref[i, s, :, span] = jnp.where(
                    row > 0,
                    pltpu.roll(x_ref[i, steps + s, :, span], 1, 0),
                    before[16 - HALO + s : 17 - HALO + s],
                )

        def first(s, state):
            made = []
            for i in range(3):
                total = tree_sum(
                    [taps_ref[i, j, :, span] * x_ref[i, s + HALO - j, :, span] for j in range(7)]
                )
                shaped[i, s, :, span] = total
                made.append(total)
            value = made[1] * made[2]
            mixed[s, :, span] = value
            return tuple(factor_ref[m, :, span] * state[m] + value for m in range(modes))

        ends = lax.fori_loop(0, steps, first, zeros)
        for m in range(modes):
            fs = jnp.broadcast_to(
                jnp.exp(-rate_row[m : m + 1, span] * float(steps)), (CHUNKS, LANES)
            )
            a = jnp.zeros((CHUNKS, LANES), f32)
            for _ in range(CHUNKS - 1):
                a = down(fs * a + ends[m])
            starts[m, :, span] = a
            fstates[block, m : m + 1, span] = (fs * a + ends[m])[CHUNKS - 1 :]

    def exchange(states, send, recv):
        return [
            remote(
                states.at[block],
                states.at[block],
                send.at[0],
                recv.at[0],
                lax.rem(block + step, count) * group + mine,
            )
            for step in range(1, count)
        ]

    forward = exchange(fstates, r["fssend"], r["fsrecv"])
    start(forward)
    for p in range(3, WPIECES):
        start(weights[p])

    acc = r["acc"]

    def upstream(j):
        if j * chunk % wide == 0:
            drain(
                wg.at[pl.ds(0, (count - 1) * own_rows), pl.ds(0, (rows_dp - 1) * strip)],
                r["precv"].at[j * chunk // wide],
            )
        cols = pl.ds(j * chunk, chunk)
        drain(gog.at[pl.ds(0, 2 * tokens), cols], r["trecv"].at[j])
        value = lax.dot_general(
            gog[:, cols], wg[:, cols], (((1,), (1,)), ((), ())), preferred_element_type=f32
        )
        acc[...] = value if j == 0 else acc[...] + value

    relay_weights(1)
    relay(0)
    relay(1)
    upstream(0)

    drain(fstates.at[pl.ds(0, count - 1)], r["fsrecv"].at[0])
    decay = jnp.exp(-rate_row[...] * float(steps * CHUNKS))
    place = row.astype(f32) * float(steps)
    incoming = jnp.zeros((modes, width), f32)
    for k in range(count):
        incoming = jnp.where(k < block, decay * incoming + fstates[k], incoming)

    gated_ref, gated_t = r["gated"], r["gated_t"]
    for n, span in enumerate(spans):
        for m in range(modes):
            rate = rate_row[m : m + 1, span]
            starts[m, :, span] += jnp.exp(-rate * place) * incoming[m : m + 1, span]

        def second(s, state):
            value = mixed[s, :, span]
            new = tuple(factor_ref[m, :, span] * state[m] + value for m in range(modes))
            filtered = tree_sum([coef_ref[m, :, span] * new[m] for m in range(modes)])
            filtered_ref[s, :, span] = filtered
            gated_ref[s, :, span] = shaped[0, s, :, span] * filtered
            return new

        lax.fori_loop(0, steps, second, tuple(starts[m, :, span] for m in range(modes)))
        gated_t[span, :] = jnp.swapaxes(
            jnp.swapaxes(gated_ref[:, :, span], 0, 1).reshape(span_tokens, LANES), 0, 1
        ).astype(bf16)
        if n == 0:
            relay(2)
            relay_weights(2)
    relay(3)

    wp, qbuf, qsum, qz, qpair = r["wp"], r["qbuf"], r["qsum"], r["qz"], r["qpair"]
    wbuf, pair, total_ref = r["wbuf"], r["pair"], r["total"]

    def product(j):
        cols = pl.ds(j * chunk, chunk)
        value = jnp.dot(gated_t[...], gog[:, cols], preferred_element_type=f32).astype(bf16)
        for k in range(count):
            wp[k, :, cols] = value[k * own_rows : (k + 1) * own_rows]

    def to_block(step):
        return lax.rem(block + step, count)

    def to_line(step):
        return lax.rem(line + step, rows_dp)

    stores = []

    def store(name, at, *where):
        src, dst = r[name], r[name + "_out"]
        if where:
            src, dst = src.at[where], dst.at[where]
        copy = pltpu.make_async_copy(src, dst, r["store"].at[at])
        copy.start()
        if not where:
            stores.append(copy)

    stages = []
    for j in range(PIECES):
        if sums_first(j):
            one = [
                remote(
                    wp.at[to_block(step), :, pl.ds(j * chunk, chunk)],
                    wbuf.at[j, step],
                    r["asend"].at[j],
                    r["arecv"].at[j],
                    to_block(step) * group + mine,
                )
                for step in range(1, count)
            ]
            two = [
                remote(
                    pair.at[j, line], pair.at[j, line],
                    r["bsend"].at[j], r["brecv"].at[j],
                    me, to_line(step),
                )
                for step in range(1, rows_dp)
            ]
            stages.append([one, two])
        else:
            one = [
                remote(
                    wp.at[
                        :, :, pl.ds(pl.multiple_of(j * chunk + to_line(step) * part, part), part)
                    ],
                    qbuf.at[j, step],
                    r["bsend"].at[j],
                    r["brecv"].at[j],
                    me,
                    to_line(step),
                )
                for step in range(1, rows_dp)
            ]
            two = [
                remote(
                    qsum.at[j, to_block(step)],
                    qz.at[j, step],
                    r["asend"].at[j],
                    r["arecv"].at[j],
                    to_block(step) * group + mine,
                )
                for step in range(1, count)
            ]
            three = [
                remote(
                    qpair.at[j, line], qpair.at[j, line],
                    r["csend"].at[j], r["crecv"].at[j],
                    me, to_line(step),
                )
                for step in range(1, rows_dp)
            ]
            stages.append([one, two, three])

    others, lines = pl.ds(1, count - 1), pl.ds(1, rows_dp - 1)

    def across_view(j):
        return wbuf.at[j, others] if sums_first(j) else qz.at[j, others]

    def lines_view(j):
        return pair.at[j, lines] if sums_first(j) else qbuf.at[j, lines]

    def reduce_one(j):
        product(j)
        start(stages[j][0])

    def reduce_two(j):
        if sums_first(j):
            drain(across_view(j), r["arecv"].at[j])
            value = wp[block, :, pl.ds(j * chunk, chunk)].astype(f32)
            for step in range(1, count):
                value = value + wbuf[j, step].astype(f32)
            pair[j, line] = value.astype(bf16)
        else:
            drain(lines_view(j), r["brecv"].at[j])
            source = pl.ds(pl.multiple_of(j * chunk + line * part, part), part)
            for k in range(count):
                value = wp[k, :, source].astype(f32)
                for step in range(1, rows_dp):
                    value = value + qbuf[j, step, k].astype(f32)
                qsum[j, k] = value.astype(bf16)
        start(stages[j][1])

    def reduce_three(j):
        if sums_first(j):
            drain(lines_view(j), r["brecv"].at[j])
            value = pair[j, 0].astype(f32)
            for other in range(1, rows_dp):
                value = value + pair[j, other].astype(f32)
            total_ref[:, pl.ds(j * chunk, chunk)] = value
            store("total", 0, slice(None), pl.ds(j * chunk, chunk))
        else:
            drain(across_view(j), r["arecv"].at[j])
            value = qsum[j, block].astype(f32)
            for step in range(1, count):
                value = value + qz[j, step].astype(f32)
            qpair[j, line] = value.astype(bf16)
            start(stages[j][2])

    def reduce_four(j):
        if not sums_first(j):
            drain(qpair.at[j, lines], r["crecv"].at[j])
            for other in range(rows_dp):
                total_ref[:, pl.ds(j * chunk + other * part, part)] = qpair[j, other].astype(f32)
            store("total", 0, slice(None), pl.ds(j * chunk, chunk))

    reduce_one(0)
    relay_weights(3)
    upstream(1)
    reduce_one(1)
    upstream(2)
    relay(4)
    reduce_one(2)
    upstream(3)
    relay(5)
    reduce_one(3)
    upstream(4)
    relay(6)
    reduce_one(4)
    upstream(5)
    reduce_one(5)
    relay(7)
    reduce_two(1)
    upstream(6)
    upstream(7)

    up_ref = r["up"]
    for span in spans:
        value = acc[:, span].reshape(CHUNKS, steps, LANES)
        up_ref[:, :, span] = jnp.swapaxes(value, 0, 1)

        def first_back(k, state):
            s = steps - 1 - k
            top = up_ref[s, :, span]
            gext[0, s, :, span] = top * filtered_ref[s, :, span]
            value = top * shaped[0, s, :, span]
            gradf[s, :, span] = value
            return tuple(factor_ref[m, :, span] * state[m] + value for m in range(modes))

        firsts = lax.fori_loop(0, steps, first_back, zeros)
        for m in range(modes):
            fs = jnp.broadcast_to(
                jnp.exp(-rate_row[m : m + 1, span] * float(steps)), (CHUNKS, LANES)
            )
            b = jnp.zeros((CHUNKS, LANES), f32)
            for _ in range(CHUNKS - 1):
                b = up(fs * b + firsts[m])
            bstarts[m, :, span] = b
            bstates[block, m : m + 1, span] = (fs * b + firsts[m])[:1]

    backward = exchange(bstates, r["bssend"], r["bsrecv"])
    start(backward)
    small_ref, edge, edge_in, y_ref = r["small"], r["edge"], r["edge_in"], r["y"]

    def edge_copy(first, size, at):
        return remote(
            edge.at[pl.ds(first, size)],
            edge_in.at[pl.ds(first, size)],
            r["esend"].at[at],
            r["erecv"].at[at],
            jnp.maximum(block - 1, 0) * group + mine,
        )

    def send_edge(first, size, at):
        for i in range(first, first + size):
            for s in range(HALO):
                edge[i, s : s + 1, :] = gext[i, s, 0:1, :]

        @pl.when(block > 0)
        def _():
            edge_copy(first, size, at).start()

    def take_edge(first, size, at):
        @pl.when(block == count - 1)
        def _():
            for i in range(first, first + size):
                edge_in[i] = jnp.zeros_like(edge_in[i])

        @pl.when(block < count - 1)
        def _():
            edge_copy(first, size, at).wait_recv()

    def tap_sums(i):
        for span in spans:

            def tap(s, sums):
                value = gext[i, s, :, span]
                return tuple(
                    sums[j] + value * x_ref[i, s + HALO - j, :, span] for j in range(7)
                )

            tapped = lax.fori_loop(0, steps, tap, zeros[:7], unroll=2)
            for j in range(7):
                at = i * 7 + j
                small_ref[at : at + 1, span] = jnp.sum(tapped[j], axis=0, keepdims=True)

    outs = []
    for i in range(3):
        outs.append([])
        for step in (2, 3, 1) if group == 4 else range(1, group):
            there = lax.rem(mine + step, group)
            outs[i].append(
                remote(
                    y_ref.at[i, there], r["yo"].at[i, mine], r["ysend"].at[0], r["yrecv"].at[i],
                    home + there,
                )
            )
    keeps = [
        pltpu.make_async_copy(y_ref.at[i, mine], r["yo"].at[i, mine], r["own"].at[1 + i])
        for i in range(3)
    ]

    def send_out(i):
        for span in spans:
            for s in range(HALO):
                gext[i, steps + s, :, span] = jnp.where(
                    row < CHUNKS - 1,
                    pltpu.roll(gext[i, s, :, span], CHUNKS - 1, 0),
                    edge_in[i, s : s + 1, span],
                )

            def out(s, nothing):
                shaped[i, s, :, span] = tree_sum(
                    [taps_ref[i, j, :, span] * gext[i, s + j, :, span] for j in range(7)]
                )
                return nothing

            lax.fori_loop(0, steps, out, 0, unroll=2)
            value = jnp.swapaxes(shaped[i, :, :, span], 0, 1).astype(bf16)
            y_ref[i, :, :, span] = value.reshape(group, tokens, LANES)
        start(outs[i])
        keeps[i].start()

    send_edge(0, 1, 0)
    reduce_two(2)
    reduce_one(6)
    reduce_one(7)
    tap_sums(0)
    reduce_two(0)
    take_edge(0, 1, 0)
    send_out(0)
    reduce_two(3)
    drain(bstates.at[pl.ds(0, count - 1)], r["bsrecv"].at[0])
    outgoing = jnp.zeros((modes, width), f32)
    for k in range(count):
        other = count - 1 - k
        outgoing = jnp.where(other > block, decay * outgoing + bstates[other], outgoing)
    far = float(steps * (CHUNKS - 1)) - place
    for n, span in enumerate(spans):
        for m in range(modes):
            rate = rate_row[m : m + 1, span]
            bstarts[m, :, span] += jnp.exp(-rate * far) * outgoing[m : m + 1, span]

        def second_back(k, carry):
            state, total = carry
            s = steps - 1 - k
            value = gradf[s, :, span]
            other = mixed[s, :, span]
            new = tuple(factor_ref[m, :, span] * state[m] + value for m in range(modes))
            total = tuple(total[m] + other * new[m] for m in range(modes))
            grad = tree_sum([coef_ref[m, :, span] * new[m] for m in range(modes)])
            gext[1, s, :, span] = grad * shaped[2, s, :, span]
            gext[2, s, :, span] = grad * shaped[1, s, :, span]
            return new, total

        _, total = lax.fori_loop(
            0, steps, second_back, (tuple(bstarts[m, :, span] for m in range(modes)), zeros)
        )
        for m in range(modes):
            small_ref[21 + m : 22 + m, span] = norm_row[m : m + 1, span] * jnp.sum(
                total[m], axis=0, keepdims=True
            )
        if n == 0:
            reduce_two(4)
    tall = small_ref.shape[0]
    if tall > 21 + modes:
        small_ref[21 + modes :, :] = jnp.zeros((tall - 21 - modes, width), f32)
    send_edge(1, 2, 1)
    tap_sums(1)
    tap_sums(2)

    sbuf, rsum, rbuf, so = r["sbuf"], r["rsum"], r["rbuf"], r["so"]
    smalls = [
        remote(
            small_ref, sbuf.at[step], r["ssend"].at[0], r["srecv"].at[0], me, to_line(step)
        )
        for step in range(1, rows_dp)
    ]
    rows = [
        remote(
            rsum, rbuf.at[step], r["rsend"].at[0], r["rrecv"].at[0],
            to_block(step) * group + mine,
        )
        for step in range(1, count)
    ]
    totals = []
    for step in range(1, group):
        there = lax.rem(mine + step, group)
        totals.append(
            remote(so.at[mine], so.at[mine], r["osend"].at[0], r["orecv"].at[0], home + there)
        )
    start(smalls)
    reduce_two(5)
    take_edge(1, 2, 1)
    send_out(1)
    reduce_two(6)
    send_out(2)

    def small_sums():
        drain(sbuf.at[lines], r["srecv"].at[0])
        total = small_ref[...]
        for step in range(1, rows_dp):
            total = total + sbuf[step]
        rsum[...] = total
        start(rows)

    def all_sums():
        drain(rbuf.at[others], r["rrecv"].at[0])
        total = rsum[...]
        for step in range(1, count):
            total = total + rbuf[step]
        so[mine] = total
        start(totals)

    small_sums()
    reduce_two(7)
    for j in range(PIECES - 1):
        reduce_three(j)
    all_sums()
    reduce_three(PIECES - 1)

    def joined(pieces):
        return jnp.concatenate(
            [
                pieces[g][:, k * own_rows : (k + 1) * own_rows]
                for k in range(count)
                for g in range(group)
            ],
            axis=1,
        )

    def take_out(i):
        drain(r["yo"].at[i, pl.ds(0, group - 1)], r["yrecv"].at[i])
        keeps[i].wait()
        name = ("gq", "gk", "gv")[i]
        r[name][...] = joined([r["yo"][i, g] for g in range(group)])
        store(name, 1 + i)

    def take_sums():
        drain(so.at[pl.ds(0, group - 1)], r["orecv"].at[0])
        sums = joined([so[g] for g in range(group)])
        for i in range(3):
            r["tap_grads"][i] = sums[7 * i : 7 * i + 7]
        r["residue_grads"][...] = sums[21 : 21 + modes]
        store("tap_grads", 4)
        store("residue_grads", 5)

    for i in range(3):
        take_out(i)
    for j in range(PIECES):
        reduce_four(j)
    take_sums()

    def settle():
        drain(xs.at[pl.ds(0, group - 1)], r["xsend"].at[0])
        for name in ("gsend", "tsend", "fsend"):
            drain(go_own, r[name].at[0])
        far_rows = pl.ds(0, (count - 1) * own_rows)
        drain(wg.at[far_rows, pl.ds(0, columns // rows_dp)], r["wsend"].at[0])
        drain(wg.at[far_rows, pl.ds(0, (rows_dp - 1) * strip * WPIECES)], r["psend"].at[0])
        drain(fstates.at[pl.ds(0, count - 1)], r["fssend"].at[0])
        drain(bstates.at[pl.ds(0, count - 1)], r["bssend"].at[0])
        for j in range(PIECES):
            drain(across_view(j), r["asend"].at[j])
            drain(lines_view(j), r["bsend"].at[j])
            if not sums_first(j):
                drain(qpair.at[j, lines], r["csend"].at[j])
        drain(sbuf.at[lines], r["ssend"].at[0])
        drain(rbuf.at[others], r["rsend"].at[0])
        drain(so.at[pl.ds(0, group - 1)], r["osend"].at[0])
        drain(y_ref.at[:, pl.ds(0, group - 1)], r["ysend"].at[0])
        drain(r["total"], r["store"].at[0])
        for copy in stores:
            copy.wait()

    settle()

    @pl.when((mine == group - 1) & (block < count - 1))
    def _():
        drain(xs.at[:, :, pl.ds(0, 16)], r["hsend"].at[0])

    @pl.when(block > 0)
    def _():
        edge_copy(0, 1, 0).wait_send()
        edge_copy(1, 2, 1).wait_send()


def finish_kernel(half, *refs):
    loaded, stored = refs[-2:]
    loads, stores = [], []
    for k in range(half):
        src, dst, held = refs[k], refs[half + k], refs[2 * half + k]
        loads.append(pltpu.make_async_copy(src, held, loaded.at[k]))
        stores.append(pltpu.make_async_copy(held, dst, stored.at[k]))
    for copy in loads:
        copy.start()
    for load, copy in zip(loads, stores):
        load.wait()
        copy.start()
    for copy in stores:
        copy.wait()


HBM = pl.BlockSpec(memory_space=pltpu.HBM)
DMA = pltpu.SemaphoreType.DMA


def shards(
    query_proj, key_proj, value_proj, grad_out, out_weight, short_taps, residues, decay_rate
):
    devices, rows_dp = lax.axis_size("ctx"), lax.axis_size("dp")
    group = math.gcd(devices, 4)
    count = devices // group
    tokens, channels = query_proj.shape[1:]
    own_rows, columns = out_weight.shape
    width = count * own_rows
    modes = residues.shape[1]
    span_tokens = group * tokens
    steps = span_tokens // CHUNKS
    f32, bf16 = jnp.float32, jnp.bfloat16
    chunk = columns // PIECES
    part = chunk // rows_dp

    rate = decay_rate.T
    norm = jnp.sqrt(-jnp.expm1(-2.0 * rate))
    coef = residues.T * norm
    tall = (21 + modes + 7) // 8 * 8
    small = (tall, width)
    scan = (steps, CHUNKS, width)
    table = (modes, CHUNKS, width)
    scratch = {
        "xs": pltpu.VMEM((group, 3, tokens, width), bf16),
        "xg": pltpu.VMEM((group, 3, tokens, width), bf16),
        "gog": pltpu.VMEM((span_tokens, columns), bf16),
        "wg": pltpu.VMEM((width, columns), bf16),
        "halo": pltpu.VMEM((3, 16, width), bf16),
        "tap_tiles": pltpu.VMEM((3, 7, CHUNKS, width), f32),
        "factor_tiles": pltpu.VMEM(table, f32),
        "coef_tiles": pltpu.VMEM(table, f32),
        "rate_rows": pltpu.VMEM((modes, width), f32),
        "norm_rows": pltpu.VMEM((modes, width), f32),
        "q": pltpu.VMEM((tokens, channels), bf16),
        "k": pltpu.VMEM((tokens, channels), bf16),
        "v": pltpu.VMEM((tokens, channels), bf16),
        "taps": pltpu.VMEM((3, 7, channels), f32),
        "factor": pltpu.VMEM((modes, channels), f32),
        "coef": pltpu.VMEM((modes, channels), f32),
        "rate": pltpu.VMEM((modes, channels), f32),
        "norm": pltpu.VMEM((modes, channels), f32),
        "x": pltpu.VMEM((3, steps + HALO, CHUNKS, width), f32),
        "shaped": pltpu.VMEM((3,) + scan, f32),
        "mixed": pltpu.VMEM(scan, f32),
        "filtered": pltpu.VMEM(scan, f32),
        "gated": pltpu.VMEM(scan, f32),
        "gradf": pltpu.VMEM(scan, f32),
        "up": pltpu.VMEM(scan, f32),
        "gext": pltpu.VMEM((3, steps + HALO, CHUNKS, width), f32),
        "starts": pltpu.VMEM(table, f32),
        "bstarts": pltpu.VMEM(table, f32),
        "fstates": pltpu.VMEM((count, modes, width), f32),
        "bstates": pltpu.VMEM((count, modes, width), f32),
        "acc": pltpu.VMEM((span_tokens, width), f32),
        "gated_t": pltpu.VMEM((width, span_tokens), bf16),
        "edge": pltpu.VMEM((3, HALO, width), f32),
        "edge_in": pltpu.VMEM((3, HALO, width), f32),
        "small": pltpu.VMEM(small, f32),
        "sbuf": pltpu.VMEM((rows_dp,) + small, f32),
        "rsum": pltpu.VMEM(small, f32),
        "rbuf": pltpu.VMEM((count,) + small, f32),
        "so": pltpu.VMEM((group,) + small, f32),
        "y": pltpu.VMEM((3, group, tokens, width), bf16),
        "yo": pltpu.VMEM((3, group, tokens, width), bf16),
        "gq": pltpu.VMEM((tokens, channels), bf16),
        "gk": pltpu.VMEM((tokens, channels), bf16),
        "gv": pltpu.VMEM((tokens, channels), bf16),
        "total": pltpu.VMEM((own_rows, columns), f32),
        "tap_grads": pltpu.VMEM((3, 7, channels), f32),
        "residue_grads": pltpu.VMEM((modes, channels), f32),
        "wp": pltpu.VMEM((count, own_rows, columns), bf16),
        "wbuf": pltpu.VMEM((PIECES, count, own_rows, chunk), bf16),
        "pair": pltpu.VMEM((PIECES, rows_dp, own_rows, chunk), bf16),
        "qbuf": pltpu.VMEM((PIECES, rows_dp, count, own_rows, part), bf16),
        "qsum": pltpu.VMEM((PIECES, count, own_rows, part), bf16),
        "qz": pltpu.VMEM((PIECES, count, own_rows, part), bf16),
        "qpair": pltpu.VMEM((PIECES, rows_dp, own_rows, part), bf16),
    }
    for name, sends, recvs in (
        ("x", 1, 1), ("g", 1, PIECES), ("t", 1, PIECES), ("w", 1, WPIECES * (count - 1)),
        ("p", 1, WPIECES), ("fs", 1, 1), ("bs", 1, 1), ("e", 2, 2),
        ("a", PIECES, PIECES), ("b", PIECES, PIECES), ("c", PIECES, PIECES),
        ("s", 1, 1), ("r", 1, 1), ("o", 1, 1), ("y", 1, 3), ("h", 1, 1),
    ):
        scratch[name + "send"] = DMA((sends,))
        scratch[name + "recv"] = DMA((recvs,))
    scratch.update(fsend=DMA((1,)), own=DMA((4,)))
    scratch["load"] = DMA((len(TABLES) + 2,))
    ins = tuple(name + "_in" for name in TABLES + ("go", "w"))
    scratch["store"] = DMA((6,))
    outs = tuple(name + "_out" for name in ("gq", "gk", "gv", "total", "tap_grads", "residue_grads"))
    grads = jax.ShapeDtypeStruct((tokens, channels), bf16)
    results = (
        grads,
        grads,
        grads,
        jax.ShapeDtypeStruct((own_rows, columns), f32),
        jax.ShapeDtypeStruct((3, 7, channels), f32),
        jax.ShapeDtypeStruct((modes, channels), f32),
    )
    made = pl.pallas_call(
        functools.partial(layer_kernel, group, count, rows_dp, ins + outs + tuple(scratch)),
        out_shape=results,
        in_specs=[HBM] * len(ins),
        out_specs=(HBM,) * len(outs),
        scratch_shapes=list(scratch.values()),
        compiler_params=pltpu.CompilerParams(
            collective_id=0, has_side_effects=True, vmem_limit_bytes=60 * 1024 * 1024
        ),
        name="layer",
    )(
        query_proj[0], key_proj[0], value_proj[0],
        jnp.swapaxes(short_taps, 1, 2), jnp.exp(-rate), coef, rate, norm,
        grad_out[0], out_weight,
    )
    gq, gk, gv, weight_grad, taps_grad, residue_grad = pl.pallas_call(
        functools.partial(finish_kernel, len(outs)),
        out_shape=results,
        in_specs=[HBM] * len(outs),
        out_specs=(HBM,) * len(outs),
        scratch_shapes=[pltpu.VMEM(v.shape, v.dtype) for v in results]
        + [DMA((len(outs),)), DMA((len(outs),))],
        compiler_params=pltpu.CompilerParams(vmem_limit_bytes=60 * 1024 * 1024),
        name="finish",
    )(*made)
    return (
        gq[None], gk[None], gv[None], weight_grad,
        jnp.swapaxes(taps_grad, 1, 2), residue_grad.T,
    )


def solution(mesh):
    placed = (
        P("dp", "ctx", None),
        P("dp", "ctx", None),
        P("dp", "ctx", None),
        P("dp", "ctx", None),
        P("ctx", None),
        P(),
        P(),
        P(),
    )
    return jax.shard_map(
        shards,
        mesh=mesh,
        in_specs=placed,
        out_specs=(
            P("dp", "ctx", None),
            P("dp", "ctx", None),
            P("dp", "ctx", None),
            P("ctx", None),
            P(),
            P(),
        ),
        check_vma=False,
    )
```
